32 devices in a mesh: gx: 4 (over z), gy: 2 (over y), gz: 4 (over x, core).
Axes of the slice: x: 2, y: 2, z: 4, core: 2. Of those that a mesh axis runs over, the one named last changes fastest.
Arguments:
- scalar_field: float32 [32, 64, 2048], P('gx', 'gy', 'gz'), may hold values from -6 to 6
- velocity: float32 [3, 32, 64, 2048], P(None, 'gx', 'gy', 'gz'), may hold values from -2.5 to 2.5
- reaction_rate: float32 [32, 64, 2048], P('gx', 'gy', 'gz'), may hold values from 0.3 to 3
- sample_cells: int32 [4, 2, 512], P('gx', 'gy', 'gz'), may hold values from 0 to 255
- weight_in: bfloat16 [3072, 1024], P(('gx', 'gy', 'gz')), may hold values from -0.1875 to 0.1875
- weight_out: bfloat16 [3072, 512], P(('gx', 'gy', 'gz')), may hold values from -0.109375 to 0.109375
Outputs:
- advanced: float32 [32, 64, 2048], P('gx', 'gy', 'gz')
- grad_in: float32 [3072, 1024], P(('gx', 'gy', 'gz'))
- grad_out: float32 [3072, 512], P(('gx', 'gy', 'gz'))
The draws below stay inside these ranges and needn't reach their ends.
All inputs are finite; a program needn't handle non-finite values.
Results may differ from the reference program's by a relative error of at most 0.0011.
Values may be sent and summed in bfloat16 or wider, within the bound.
A program may use at most 64 MiB of HBM per device.

```python
import math
import jax
import jax.numpy as jnp
from jax import lax

CX = 8
CY = 32
PEN = 512
IN = 1024
HID = 3072
S_DEV = 128
STEPS = 3
SAMPLES = 4096
NX = 32
NY = 64
NZ = 2048
N_GX = 4
N_GY = 2
N_GZ = 4


def with_ends(values, key, smallest, high):
    place = [jax.random.randint(jax.random.fold_in(key, axis), (), 0, length) for axis, length in enumerate(values.shape)]
    main_axis = values.shape.index(max(values.shape))
    neighbour = place[:main_axis] + [(place[main_axis] + 1) % values.shape[main_axis]] + place[main_axis + 1:]
    return values.at[tuple(place)].set(smallest).at[tuple(neighbour)].set(high)


def block_levels(rng, shape, pieces, least, top_value):
    def one(axis_at, blocks):
        heights = jax.random.uniform(jax.random.fold_in(jax.random.fold_in(rng, 6), axis_at), (blocks,), jnp.float32, least / len(pieces), top_value / len(pieces))
        return jnp.repeat(jnp.exp(heights), shape[axis_at] // blocks).reshape((-1,) + (1,) * (len(shape) - axis_at - 1))

    factor_of = one(*pieces[0])
    for cut in pieces[1:]:
        factor_of = factor_of * one(*cut)
    return factor_of


def normal_values(stream_key, shape, spread, limit, cuts=(), held_as=jnp.bfloat16):
    result = jax.random.normal(stream_key, shape, jnp.float32) * spread
    if len(cuts) > 0:
        result = block_levels(stream_key, shape, cuts, -0.22, 0.18) * result
    return jnp.clip(result, min=-limit, max=limit).astype(held_as)


def setup_inputs(seed: int = 0) -> dict:
    streams_of = jax.random.split(jax.random.key(seed), 7)
    return {
        "scalar_field": normal_values(streams_of[0], (NX, NY, NZ), 1.0, 6.0, ((0, 4), (1, 2), (2, 4)), jnp.float32),
        "velocity": normal_values(streams_of[1], (3, NX, NY, NZ), 0.4, 2.5, ((1, 4), (2, 2), (3, 4)), jnp.float32),
        "reaction_rate": jnp.clip(jnp.exp(math.log(3.0) - 2.3025851 * jax.random.uniform(streams_of[2], (NX, NY, NZ), jnp.float32) ** block_levels(streams_of[2], (NX, NY, NZ), ((0, 4), (1, 2), (2, 4)), -0.2, 0.2)), 0.3, 3.0),
        "sample_cells": with_ends(jax.random.randint(streams_of[3], (N_GX, N_GY, N_GZ * S_DEV), 0, CX * CY), jax.random.fold_in(streams_of[3], 1), 0, (CX * CY) - 1).astype(jnp.int32),
        "weight_in": normal_values(streams_of[4], (HID, IN), IN ** -0.5, 0.1875, ((0, 32),)),
        "weight_out": normal_values(streams_of[5], (HID, PEN), HID ** -0.5, 0.109375, ((0, 32),)),
    }


TIME_STEP = 0.15


def update(field, velocity, reaction_rate):
    x_plus = jnp.roll(field, -1, 0)
    x_minus = jnp.roll(field, 1, 0)
    y_plus = jnp.roll(field, -1, 1)
    y_minus = jnp.roll(field, 1, 1)
    z_plus = jnp.roll(field, -1, 2)
    z_minus = jnp.roll(field, 1, 2)
    laplace = (x_plus + x_minus) + (y_plus + y_minus) + (z_plus + z_minus) - 6.0 * field
    advect = velocity[0] * (x_plus - x_minus) + velocity[1] * (y_plus - y_minus) + velocity[2] * (z_plus - z_minus)
    return field + TIME_STEP * (laplace - 0.5 * advect - reaction_rate * field)


def dsilu(value):
    sig = jax.nn.sigmoid(value)
    return sig * (1.0 + value * (1.0 - sig))


def blocks_of(field):
    shaped = field.reshape(N_GX, CX, N_GY, CY, N_GZ, PEN)
    return shaped.transpose(0, 2, 4, 1, 3, 5).reshape(N_GX * N_GY * N_GZ, CX * CY, PEN)


def reference(scalar_field, velocity, reaction_rate, sample_cells, weight_in, weight_out):
    snaps = []
    current = scalar_field
    for step_num in range(STEPS):
        current = update(current, velocity, reaction_rate)
        snaps.append(current)
    first = blocks_of(snaps[0])
    second = blocks_of(snaps[1])
    third = blocks_of(snaps[2])
    picks = sample_cells.reshape(N_GX, N_GY, N_GZ, S_DEV).reshape(N_GX * N_GY * N_GZ, S_DEV).astype(jnp.int32)
    scale = 1.0 / (float(SAMPLES) ** 0.5)
    contract_last = (((1,), (1,)), ((), ()))
    contract_first = (((0,), (0,)), ((), ()))

    def one_block(carry, block):
        first_b, second_b, third_b, pick_b = block
        inputs = jnp.concatenate([jnp.take(first_b, pick_b, axis=0), jnp.take(second_b, pick_b, axis=0)], 1).astype(jnp.bfloat16)
        target = jnp.take(third_b, pick_b, axis=0)
        preact = lax.dot_general(inputs, weight_in, contract_last, preferred_element_type=jnp.float32)
        hidden = jax.nn.silu(preact).astype(jnp.bfloat16)
        predict = jnp.dot(hidden, weight_out, preferred_element_type=jnp.float32)
        resid = ((predict - target) * scale).astype(jnp.bfloat16)
        back = lax.dot_general(resid, weight_out, contract_last, preferred_element_type=jnp.float32)
        dpre = (back * dsilu(preact)).astype(jnp.bfloat16)
        g_in = carry[0] + lax.dot_general(dpre, inputs, contract_first, preferred_element_type=jnp.float32)
        g_out = carry[1] + lax.dot_general(hidden, resid, contract_first, preferred_element_type=jnp.float32)
        return (g_in, g_out), None

    start = (jnp.zeros((HID, IN), jnp.float32), jnp.zeros((HID, PEN), jnp.float32))
    (grad_in, grad_out), unused = lax.scan(one_block, start, (first, second, third, picks))
    return snaps[2], grad_in, grad_out
```

```python
import functools
import math

import jax
import jax.numpy as jnp
from jax import lax
from jax.experimental import pallas as pl
from jax.experimental.pallas import tpu as pltpu
from jax.sharding import PartitionSpec as P

STEPS = 3
TIME_STEP = 0.15
HALVES = 2
NT = (((1,), (1,)), ((), ()))
TN = (((0,), (0,)), ((), ()))
F32 = jnp.float32
BF16 = jnp.bfloat16
I16 = jnp.int16
TOP = 32766.0
TINY = 1e-30


def mm(a, b, dims=None):
    if dims is None:
        return jnp.dot(a, b, preferred_element_type=F32)
    return lax.dot_general(a, b, dims, preferred_element_type=F32)


def log2(n):
    bits = n.bit_length() - 1
    assert 1 << bits == n
    return bits


def encode(x):
    top = jnp.maximum(jnp.max(jnp.abs(x), axis=0, keepdims=True), TINY)
    return jnp.round(x * (TOP / top)).astype(I16), top * (1.0 / TOP)


def decode(q, unit):
    return q.astype(F32) * unit


def kernel(
    sizes, scale, widths,
    u_ref, vel_ref, rate_ref, picks_ref, win_ref, wout_ref,
    adv_ref, gin_ref, gout_ref,
    snaps, vel, rate, hx, hy_out, hy, hz_out, hz, hot_t, xin, wts, pre, hid, pf, tgt,
    p_out, p_in, p_unit_out, p_unit_in, res, g, core_in, q_out, q_in, u_out, u_in,
    halo_s, halo_r, x_s, x_r, w_s, w_r, p_s, p_r, r_s, r_r, g_s, g_r, loc,
):
    T, NY, NZ = sizes
    gx, gy, gz = lax.axis_index("gx"), lax.axis_index("gy"), lax.axis_index("gz")
    CX, CY, PEN = vel.shape[1:]
    rows = CX * CY
    S = hot_t.shape[0]
    S2 = S // HALVES
    Hc, IN = win_ref.shape
    NI = IN // PEN
    NE = NY * 2
    gxh, gxl = gx // 2, gx % 2
    me_e = gy * 2 + gxl
    wbits = [("gz", b) for b in range(log2(NZ))] + [("gx", b) for b in range(1, log2(T))]
    nw = len(wbits)
    NW = 1 << nw
    index = {"gx": gx, "gy": gy, "gz": gz}
    mb = [(index[a] // (1 << b)) % 2 for a, b in wbits]
    me_w = sum(mb[i] * (1 << (nw - 1 - i)) for i in range(nw))

    def w_partner(i):
        a, b = wbits[i]
        return {a: index[a] + (1 - 2 * mb[i]) * (1 << b)}

    e_pairs = []
    for dy in range(NY):
        for dx in range(2):
            if dy or dx:
                lo = (gxl + dx) % 2
                to = {"gy": (gy + dy) % NY, "gx": gxh * 2 + lo}
                e_pairs.append((to, ((gy + dy) % NY) * 2 + lo, ((gy + NY - dy) % NY) * 2 + lo))
    e_pairs = e_pairs[::-1]
    NP = NE - 1

    sides = [
        ({"gx": (gx + 1) % T}, {"gx": (gx + T - 1) % T}),
        ({"gy": (gy + 1) % NY}, {"gy": (gy + NY - 1) % NY}),
        ({"gz": (gz + 1) % NZ}, {"gz": (gz + NZ - 1) % NZ}),
    ]

    def remote(src, dst, ss, rs, dev):
        return pltpu.make_async_remote_copy(
            src_ref=src, dst_ref=dst, send_sem=ss, recv_sem=rs,
            device_id=dev, device_id_type=pl.DeviceIdType.MESH,
        )

    load_u = pltpu.make_async_copy(u_ref, snaps.at[0], loc.at[0])
    load_v = pltpu.make_async_copy(vel_ref, vel, loc.at[1])
    load_r = pltpu.make_async_copy(rate_ref, rate, loc.at[2])
    NM = NI + 1
    sources = [win_ref.at[:, pl.ds(i * PEN, PEN)] for i in range(NI)] + [wout_ref]
    load_w = [pltpu.make_async_copy(sources[i], wts.at[i, me_w], loc.at[3 + i]) for i in range(NM)]
    load_u.start()
    load_v.start()
    load_r.start()
    for c in load_w:
        c.start()

    barrier = pltpu.get_barrier_semaphore()
    greet = [p[0] for p in e_pairs] + [w_partner(i) for i in range(nw)]
    for pair in sides:
        greet += list(pair)
    for dev in greet:
        pl.semaphore_signal(barrier, inc=1, device_id=dev, device_id_type=pl.DeviceIdType.MESH)
    pl.semaphore_wait(barrier, len(greet))

    def w_copy(m, stage):
        i = nw - 1 - stage
        size = 1 << stage
        base = sum(mb[j] * (1 << (nw - 1 - j)) for j in range(i + 1))
        theirs = base + (1 - 2 * mb[i]) * size
        sems = (w_s.at[m, stage], w_r.at[m, stage])
        if stage == 0:
            send = remote(sources[m], wts.at[m, me_w], *sems, w_partner(i))
        else:
            mine = wts.at[m, pl.ds(base, size)]
            send = remote(mine, mine, *sems, w_partner(i))
        other = wts.at[m, pl.ds(theirs, size)]
        recv = remote(other, other, *sems, w_partner(i))
        return send, recv

    def w_start(m, stage):
        if stage == 1:
            load_w[m].wait()
        w_copy(m, stage)[0].start()

    def w_wait(m, stage):
        w_copy(m, stage)[1].wait_recv()

    def w_next(m, stage):
        if stage <= nw:
            w_wait(m, stage - 1)
        if stage < nw:
            w_start(m, stage)

    def halo(step):
        cur = u_ref if step == 0 else snaps.at[step]
        faces = [
            (cur.at[pl.ds(rows - CY, CY)], hx.at[step, 0], sides[0][0]),
            (cur.at[pl.ds(0, CY)], hx.at[step, 1], sides[0][1]),
            (hy_out.at[step, 0], hy.at[step, 0], sides[1][0]),
            (hy_out.at[step, 1], hy.at[step, 1], sides[1][1]),
            (hz_out.at[step, 0], hz.at[step, 0], sides[2][0]),
            (hz_out.at[step, 1], hz.at[step, 1], sides[2][1]),
        ]
        return [
            remote(s, d, halo_s.at[step, i], halo_r.at[step, i], dev)
            for i, (s, d, dev) in enumerate(faces)
        ]

    lane = lax.broadcasted_iota(jnp.int32, (CY, 128), 1)

    def halo_x(step):
        for c in halo(step)[:2]:
            c.start()

    def halo_yz(step):
        copies = halo(step)
        lo = jnp.zeros((CY, 128), F32)
        hi = jnp.zeros((CY, 128), F32)
        for i in range(CX):
            hy_out[step, 0, pl.ds(i, 1), :] = snaps[step, pl.ds(i * CY + CY - 1, 1), :]
            hy_out[step, 1, pl.ds(i, 1), :] = snaps[step, pl.ds(i * CY, 1), :]
            last = snaps[step, pl.ds(i * CY, CY), pl.ds(PEN - 128, 128)]
            head = snaps[step, pl.ds(i * CY, CY), pl.ds(0, 128)]
            hi = jnp.where(lane == i, pltpu.roll(last, i + 1, 1), hi)
            lo = jnp.where(lane == i, pltpu.roll(head, i, 1) if i else head, lo)
        hz_out[step, 0] = hi
        hz_out[step, 1] = lo
        for c in copies[2:]:
            c.start()

    row_id = lax.broadcasted_iota(jnp.int32, (CY, PEN), 0)
    lane_id = lax.broadcasted_iota(jnp.int32, (CY, PEN), 1)

    def layer(step, i):
        if i < 0:
            return hx[step, 0]
        if i >= CX:
            return hx[step, 1]
        return snaps[step, pl.ds(i * CY, CY), :]

    def advance(step, i):
        u = layer(step, i)
        xp, xm = layer(step, i + 1), layer(step, i - 1)
        yp = jnp.where(row_id == CY - 1, hy[step, 1, pl.ds(i, 1), :], pltpu.roll(u, CY - 1, 0))
        ym = jnp.where(row_id == 0, hy[step, 0, pl.ds(i, 1), :], pltpu.roll(u, 1, 0))
        zhi = hz[step, 1][:, i:i + 1]
        zlo = hz[step, 0][:, i:i + 1]
        zp = jnp.where(lane_id == PEN - 1, zhi, pltpu.roll(u, PEN - 1, 1))
        zm = jnp.where(lane_id == 0, zlo, pltpu.roll(u, 1, 1))
        lap = (xp + xm) + (yp + ym) + (zp + zm) - 6.0 * u
        adv = vel[0, i] * (xp - xm) + vel[1, i] * (yp - ym) + vel[2, i] * (zp - zm)
        new = u + TIME_STEP * (lap - 0.5 * adv - rate[i] * u)
        snaps[step + 1, pl.ds(i * CY, CY), :] = new

    def inner(step):
        for c in halo(step)[2:]:
            c.wait_recv()
        for i in range(1, CX - 1):
            advance(step, i)

    def outer(step):
        for c in halo(step)[:2]:
            c.wait_recv()
        for i in sorted({0, CX - 1}):
            advance(step, i)

    def x_copy(n, h, k):
        to, _, src = e_pairs[k]
        cols = pl.ds(n * PEN, PEN)
        sems = (x_s.at[n, h, k], x_r.at[n, h, k])
        mine, other = xin.at[h, me_e, :, cols], xin.at[h, src, :, cols]
        return remote(mine, mine, *sems, to), remote(other, other, *sems, to)

    def gather(n):
        snap = snaps[n + 1].astype(BF16)
        for h in range(HALVES):
            picked = mm(hot_t[pl.ds(h * S2, S2)], snap).astype(BF16)
            xin[h, me_e, :, pl.ds(n * PEN, PEN)] = picked
            for k in range(NP):
                x_copy(n, h, k)[0].start()

    def x_wait(n, h):
        for k in range(NP):
            x_copy(n, h, k)[1].wait_recv()

    halo_x(0)
    w_start(0, 0)
    load_u.wait()
    halo_yz(0)
    hot = jnp.where(
        lax.broadcasted_iota(jnp.int32, (rows, S), 0) == picks_ref[...], 1.0, 0.0
    )
    hot_t[...] = jnp.transpose(hot).astype(BF16)
    load_v.wait()
    load_r.wait()
    inner(0)
    outer(0)
    halo_x(1)
    halo_yz(1)
    gather(0)
    w_start(1, 0)
    w_next(0, 1)
    inner(1)
    outer(1)
    halo_x(2)
    halo_yz(2)
    gather(1)
    for m in range(2, NM):
        w_start(m, 0)
    w_next(1, 1)
    w_next(0, 2)
    inner(2)
    outer(2)
    snap3 = snaps[STEPS]
    adv_ref[...] = snap3.reshape(CX, CY, PEN)
    hi = snap3.astype(BF16)
    rest = snap3 - hi.astype(F32)
    mid = rest.astype(BF16)
    low = (rest - mid.astype(F32)).astype(BF16)
    ht = hot_t[...]
    tgt[...] = (mm(ht, hi) + mm(ht, mid)) + mm(ht, low)
    for m in range(2, NM):
        w_next(m, 1)
    w_next(1, 2)
    for stage in range(3, nw + 1):
        w_next(0, stage)

    SH = NE * S2
    cb = 4 if NW % 4 == 0 else NW
    HB = cb * Hc
    NB = NW // cb

    def weight(m, b):
        return wts[m, pl.ds(b * cb, cb)].reshape(HB, PEN)

    def x_half(h, n):
        return xin[h, :, :, pl.ds(n * PEN, PEN)].reshape(SH, PEN)

    for h in range(HALVES):
        x_wait(0, h)
        for b in range(NB):
            pre[h, pl.ds(b * cb, cb)] = mm(weight(0, b), x_half(h, 0), NT).reshape(cb, Hc, SH)
    for m in range(2, NM):
        w_next(m, 2)
    for stage in range(3, nw + 1):
        w_next(1, stage)

    def p_copies(h, k):
        to = e_pairs[k][0]
        return (
            remote(p_out.at[h, k], p_in.at[h, k], p_s.at[0, h, k], p_r.at[0, h, k], to),
            remote(p_unit_out.at[h, k], p_unit_in.at[h, k], p_s.at[1, h, k], p_r.at[1, h, k], to),
        )

    for h in range(HALVES):
        x_wait(1, h)
        for b in range(NB):
            blk = pl.ds(b * cb, cb)
            v = pre[h, blk].reshape(HB, SH) + mm(weight(1, b), x_half(h, 1), NT)
            pre[h, blk] = v.reshape(cb, Hc, SH)
            hid[h, blk] = (v / (1.0 + jnp.exp(-v))).astype(BF16).reshape(cb, Hc, SH)
        if h == 0:
            for m in range(2, NM):
                for stage in range(3, nw + 1):
                    w_next(m, stage)
        pf[h] = mm(
            hid[h].reshape(NW * Hc, SH), wts[NI].reshape(NW * Hc, PEN), TN
        ).reshape(NE, S2, PEN)
        for k in range(NP):
            q, unit = encode(pf[h, e_pairs[k][1]])
            p_out[h, k] = q
            p_unit_out[h, k] = unit
            for c in p_copies(h, k):
                c.start()

    def r_copy(h, k):
        to, _, src = e_pairs[k]
        sems = (r_s.at[h, k], r_r.at[h, k])
        mine, other = res.at[h, me_e], res.at[h, src]
        return remote(mine, mine, *sems, to), remote(other, other, *sems, to)

    for h in range(HALVES):
        total = pf[h, me_e] - tgt[pl.ds(h * S2, S2), :]
        for k in range(NP):
            for c in p_copies(h, k):
                c.wait_recv()
            total = total + decode(p_in[h, k], p_unit_in[h, k])
        res[h, me_e] = (total * scale).astype(BF16)
        for k in range(NP):
            r_copy(h, k)[0].start()

    for h in range(HALVES):
        for b in range(NB):
            blk = pl.ds(b * cb, cb)
            v = pre[h, blk]
            sig = 1.0 / (1.0 + jnp.exp(-v))
            pre[h, blk] = sig * (1.0 + v * (1.0 - sig))

    starts = [sum(widths[:c]) for c in range(len(widths))]

    def cols_of(c):
        return pl.ds(starts[c], widths[c])

    def q_rows(stage):
        return sum((NW >> (s + 1)) for s in range(1, stage))

    def core_copy(c):
        half = NW // 2
        return remote(
            g.at[pl.ds((1 - mb[0]) * half, half), :, cols_of(c)], core_in.at[:, :, cols_of(c)],
            g_s.at[0, 0, c], g_r.at[0, 0, c], w_partner(0),
        )

    def stage_copies(c, stage):
        size = NW >> (stage + 1)
        blk = pl.ds(q_rows(stage), size)
        one = pl.ds(stage - 1, 1)
        return (
            remote(q_out.at[blk, :, cols_of(c)], q_in.at[blk, :, cols_of(c)],
                   g_s.at[stage, 0, c], g_r.at[stage, 0, c], w_partner(stage)),
            remote(u_out.at[one, :, cols_of(c)], u_in.at[one, :, cols_of(c)],
                   g_s.at[stage, 1, c], g_r.at[stage, 1, c], w_partner(stage)),
        )

    def base_of(stage):
        return sum(mb[j] * (1 << (nw - 1 - j)) for j in range(stage))

    def put(c, val):
        g[:, :, cols_of(c)] = val.reshape(NW, Hc, widths[c])
        core_copy(c).start()

    def reduce(c, stage):
        size = NW >> (stage + 1)
        W = widths[c]
        flat = size * Hc
        if stage == 0:
            core_copy(c).wait_recv()

            def came(off, n):
                return core_in[pl.ds(off, n), :, cols_of(c)].reshape(n * Hc, W)
        else:
            for cp in stage_copies(c, stage):
                cp.wait_recv()
            unit = u_in[stage - 1, :, cols_of(c)]

            def came(off, n):
                return decode(q_in[pl.ds(q_rows(stage) + off, n), :, cols_of(c)].reshape(n * Hc, W), unit)
        base = base_of(stage + 1)
        if size == 1:
            val = g[base, :, cols_of(c)] + came(0, 1)
            if starts[c] < PEN:
                gout_ref[:, cols_of(c)] = val
            else:
                gin_ref[:, pl.ds(starts[c] - PEN, W)] = val
            return
        half = size // 2
        nxt = mb[stage + 1]
        away, keep = (1 - nxt) * half, nxt * half
        val = g[pl.ds(base + away, half), :, cols_of(c)].reshape(half * Hc, W) + came(away, half)
        q, unit_out = encode(val)
        q_out[pl.ds(q_rows(stage + 1), half), :, cols_of(c)] = q.reshape(half, Hc, W)
        u_out[stage, :, cols_of(c)] = unit_out
        for cp in stage_copies(c, stage + 1):
            cp.start()
        val = g[pl.ds(base + keep, half), :, cols_of(c)].reshape(half * Hc, W) + came(keep, half)
        g[pl.ds(base + keep, half), :, cols_of(c)] = val.reshape(half, Hc, W)

    C = len(widths)
    first = [c for c in range(C) if starts[c] < PEN]

    for h in range(HALVES):
        for k in range(NP):
            r_copy(h, k)[1].wait_recv()
    for i, c in enumerate(first):
        val = None
        for h in range(HALVES):
            r = res[h, :, :, cols_of(c)].reshape(SH, widths[c])
            term = mm(hid[h].reshape(NW * Hc, SH), r)
            val = term if val is None else val + term
        put(c, val)
    for h in range(HALVES):
        for b in range(NB):
            blk = pl.ds(b * cb, cb)
            back = mm(weight(NI, b), res[h].reshape(SH, PEN), NT)
            hid[h, blk] = (back * pre[h, blk].reshape(HB, SH)).astype(BF16).reshape(cb, Hc, SH)
    reduced = 0
    for c in range(len(first), C):
        val = None
        for h in range(HALVES):
            x = xin[h, :, :, pl.ds(starts[c] - PEN, widths[c])].reshape(SH, widths[c])
            term = mm(hid[h].reshape(NW * Hc, SH), x)
            val = term if val is None else val + term
        put(c, val)
        if reduced < c - 1:
            reduce(reduced, 0)
            reduced += 1
    while reduced < C:
        reduce(reduced, 0)
        reduced += 1
    lag = 2
    for t in range(C + lag * nw):
        for stage in range(1, nw):
            c = t - lag * (stage - 1)
            if 0 <= c < C:
                reduce(c, stage)

    for step in range(STEPS):
        for cp in halo(step):
            cp.wait_send()
    for m in range(NM):
        if nw == 1:
            load_w[m].wait()
        for stage in range(nw):
            w_copy(m, stage)[0].wait_send()
    for h in range(HALVES):
        for k in range(NP):
            for n in range(NI):
                x_copy(n, h, k)[0].wait_send()
            for cp in p_copies(h, k):
                cp.wait_send()
            r_copy(h, k)[0].wait_send()
    for c in range(C):
        core_copy(c).wait_send()
        for stage in range(1, nw):
            for cp in stage_copies(c, stage):
                cp.wait_send()


def shards(sizes, scalar_field, velocity, reaction_rate, sample_cells, weight_in, weight_out):
    T, NY, NZ = sizes
    NE = NY * 2
    NW = NZ * (T // 2)
    NP = NE - 1
    nw = log2(NW)
    CX, CY, PEN = scalar_field.shape
    S = sample_cells.shape[-1]
    S2 = S // HALVES
    SH = NE * S2
    Hc, IN = weight_in.shape
    NI = IN // PEN
    NM = NI + 1
    wide = IN + PEN
    W = PEN // 2
    widths = (W,) * (wide // W - 1) + (W // 2,) * 2
    C = len(widths)
    scale = 1.0 / math.sqrt(S * T * NY * NZ)
    rows = CX * CY
    dma = pltpu.SemaphoreType.DMA
    vmem = pl.BlockSpec(memory_space=pltpu.VMEM)
    hbm = pl.BlockSpec(memory_space=pltpu.HBM)
    shapes = ((CX, CY, PEN), (Hc, IN), (Hc, PEN))
    return tuple(pl.pallas_call(
        functools.partial(kernel, sizes, scale, widths),
        out_shape=tuple(pltpu.VMEM(s, F32) for s in shapes),
        in_specs=[hbm, hbm, hbm, vmem, hbm, hbm],
        out_specs=(vmem,) * 3,
        scratch_shapes=[
            pltpu.VMEM((STEPS + 1, rows, PEN), F32),
            pltpu.VMEM((3, CX, CY, PEN), F32),
            pltpu.VMEM((CX, CY, PEN), F32),
            pltpu.VMEM((STEPS, 2, CY, PEN), F32),
            pltpu.VMEM((STEPS, 2, CX, PEN), F32),
            pltpu.VMEM((STEPS, 2, CX, PEN), F32),
            pltpu.VMEM((STEPS, 2, CY, 128), F32),
            pltpu.VMEM((STEPS, 2, CY, 128), F32),
            pltpu.VMEM((S, rows), BF16),
            pltpu.VMEM((HALVES, NE, S2, IN), BF16),
            pltpu.VMEM((NM, NW, Hc, PEN), BF16),
            pltpu.VMEM((HALVES, NW, Hc, SH), F32),
            pltpu.VMEM((HALVES, NW, Hc, SH), BF16),
            pltpu.VMEM((HALVES, NE, S2, PEN), F32),
            pltpu.VMEM((S, PEN), F32),
            pltpu.VMEM((HALVES, NP, S2, PEN), I16),
            pltpu.VMEM((HALVES, NP, S2, PEN), I16),
            pltpu.VMEM((HALVES, NP, 1, PEN), F32),
            pltpu.VMEM((HALVES, NP, 1, PEN), F32),
            pltpu.VMEM((HALVES, NE, S2, PEN), BF16),
            pltpu.VMEM((NW, Hc, wide), F32),
            pltpu.VMEM((NW // 2, Hc, wide), F32),
            pltpu.VMEM((NW // 2 - 1, Hc, wide), I16),
            pltpu.VMEM((NW // 2 - 1, Hc, wide), I16),
            pltpu.VMEM((nw - 1, 1, wide), F32),
            pltpu.VMEM((nw - 1, 1, wide), F32),
            dma((STEPS, 6)), dma((STEPS, 6)),
            dma((NI, HALVES, NP)), dma((NI, HALVES, NP)),
            dma((NM, nw)), dma((NM, nw)),
            dma((2, HALVES, NP)), dma((2, HALVES, NP)),
            dma((HALVES, NP)), dma((HALVES, NP)),
            dma((nw, 2, C)), dma((nw, 2, C)),
            dma((3 + NM,)),
        ],
        compiler_params=pltpu.CompilerParams(
            collective_id=0, has_side_effects=True, vmem_limit_bytes=56 * 1024 * 1024
        ),
    )(
        scalar_field.reshape(rows, PEN), velocity, reaction_rate,
        sample_cells.reshape(1, S), weight_in, weight_out,
    ))


def solution(mesh):
    sizes = (mesh.shape["gx"], mesh.shape["gy"], mesh.shape["gz"])
    in_specs = (
        P("gx", "gy", "gz"),
        P(None, "gx", "gy", "gz"),
        P("gx", "gy", "gz"),
        P("gx", "gy", "gz"),
        P(("gx", "gy", "gz"), None),
        P(("gx", "gy", "gz"), None),
    )
    out_specs = (P("gx", "gy", "gz"), P(("gx", "gy", "gz"), None), P(("gx", "gy", "gz"), None))
    return jax.shard_map(
        functools.partial(shards, sizes), mesh=mesh, in_specs=in_specs, out_specs=out_specs,
        check_vma=False,
    )
```

```python
import functools
import math

import jax
import jax.numpy as jnp
from jax import lax
from jax.experimental import pallas as pl
from jax.experimental.pallas import tpu as pltpu
from jax.sharding import PartitionSpec as P

STEPS = 3
FIRST, SECOND, EARLY = 3, 6, True
TIME_STEP = 0.15
PARTS = 2
NT = (((1,), (1,)), ((), ()))
TN = (((0,), (0,)), ((), ()))
F32 = jnp.float32
BF16 = jnp.bfloat16
I16 = jnp.int16
TOP = 32766.0
TINY = 1e-30


def mm(a, b, dims=None):
    if dims is None:
        return jnp.dot(a, b, preferred_element_type=F32)
    return lax.dot_general(a, b, dims, preferred_element_type=F32)


def log2(n):
    bits = n.bit_length() - 1
    assert 1 << bits == n
    return bits


def encode(x):
    top = jnp.maximum(jnp.max(jnp.abs(x), axis=0, keepdims=True), TINY)
    return jnp.round(x * (TOP / top)).astype(I16), top * (1.0 / TOP)


def decode(q, unit):
    return q.astype(F32) * unit


def kernel(
    sizes, scale, widths,
    u_ref, vel_ref, rate_ref, picks_ref, win_ref, wout_ref,
    adv_ref, gin_ref, gout_ref,
    snaps, vel, rate, hx, hy_out, hy, hz_out, hz, hot_t, xin, wts, pre, hid, pf, tgt,
    p_out, p_in, p_unit_out, p_unit_in, res, g, core_in, q_out, q_in, u_out, u_in,
    halo_s, halo_r, x_s, x_r, w_s, w_r, p_s, p_r, r_s, r_r, g_s, g_r, loc,
):
    T, NY, NZ = sizes
    gx, gy, gz = lax.axis_index("gx"), lax.axis_index("gy"), lax.axis_index("gz")
    CX, CY, PEN = vel.shape[1:]
    rows = CX * CY
    S = hot_t.shape[0]
    Hc, IN = win_ref.shape
    NI = IN // PEN
    NE = NY * 2
    gxh, gxl = gx // 2, gx % 2
    me_e = gy * 2 + gxl
    wbits = [("gz", b) for b in range(log2(NZ))] + [("gx", b) for b in range(1, log2(T))]
    nw = len(wbits)
    NW = 1 << nw
    index = {"gx": gx, "gy": gy, "gz": gz}
    mb = [(index[a] // (1 << b)) % 2 for a, b in wbits]
    me_w = sum(mb[i] * (1 << (nw - 1 - i)) for i in range(nw))

    def w_partner(i):
        a, b = wbits[i]
        return {a: index[a] + (1 - 2 * mb[i]) * (1 << b)}

    e_pairs = []
    for dy in range(NY):
        for dx in range(2):
            if dy or dx:
                lo = (gxl + dx) % 2
                to = {"gy": (gy + dy) % NY, "gx": gxh * 2 + lo}
                e_pairs.append((to, ((gy + dy) % NY) * 2 + lo, ((gy + NY - dy) % NY) * 2 + lo))
    e_pairs = e_pairs[::-1]
    NP = NE - 1

    sides = [
        ({"gx": (gx + 1) % T}, {"gx": (gx + T - 1) % T}),
        ({"gy": (gy + 1) % NY}, {"gy": (gy + NY - 1) % NY}),
        ({"gz": (gz + 1) % NZ}, {"gz": (gz + NZ - 1) % NZ}),
    ]

    def remote(src, dst, ss, rs, dev):
        return pltpu.make_async_remote_copy(
            src_ref=src, dst_ref=dst, send_sem=ss, recv_sem=rs,
            device_id=dev, device_id_type=pl.DeviceIdType.MESH,
        )

    load_u = pltpu.make_async_copy(u_ref, snaps.at[0], loc.at[0])
    load_v = pltpu.make_async_copy(vel_ref, vel, loc.at[1])
    load_r = pltpu.make_async_copy(rate_ref, rate, loc.at[2])
    NM = NI + 1
    sources = [win_ref.at[:, pl.ds(i * PEN, PEN)] for i in range(NI)] + [wout_ref]
    load_w = [pltpu.make_async_copy(sources[i], wts.at[i, me_w], loc.at[3 + i]) for i in range(NM)]
    load_u.start()
    load_v.start()
    load_r.start()
    for c in load_w:
        c.start()

    barrier = pltpu.get_barrier_semaphore()
    greet = [p[0] for p in e_pairs] + [w_partner(i) for i in range(nw)]
    for pair in sides:
        greet += list(pair)
    for dev in greet:
        pl.semaphore_signal(barrier, inc=1, device_id=dev, device_id_type=pl.DeviceIdType.MESH)
    pl.semaphore_wait(barrier, len(greet))

    WP = PEN // PARTS
    pieces = [(m, part) for m in range(NM) for part in range(PARTS)]

    def w_copy(n, stage):
        m, part = pieces[n]
        cols = pl.ds(part * WP, WP)
        i = nw - 1 - stage
        size = 1 << stage
        base = sum(mb[j] * (1 << (nw - 1 - j)) for j in range(i + 1))
        theirs = base + (1 - 2 * mb[i]) * size
        sems = (w_s.at[n, stage], w_r.at[n, stage])
        if stage == 0:
            src = win_ref.at[:, pl.ds(m * PEN + part * WP, WP)] if m < NI else wout_ref.at[:, cols]
            send = remote(src, wts.at[m, me_w, :, cols], *sems, w_partner(i))
        else:
            mine = wts.at[m, pl.ds(base, size), :, cols]
            send = remote(mine, mine, *sems, w_partner(i))
        other = wts.at[m, pl.ds(theirs, size), :, cols]
        recv = remote(other, other, *sems, w_partner(i))
        return send, recv

    def w_start(n, stage):
        if stage == 1 and n % PARTS == 0:
            load_w[n // PARTS].wait()
        w_copy(n, stage)[0].start()

    def w_next(n, stage):
        w_copy(n, stage - 1)[1].wait_recv()
        if stage < nw:
            w_start(n, stage)

    def w_inner(group):
        for n in group:
            for stage in range(2, nw):
                w_next(n, stage)

    def w_last(group):
        if nw > 1:
            for n in group:
                w_next(n, nw)

    NQ = len(pieces)
    of_in0 = range(PARTS)
    of_in1 = range(PARTS, NI * PARTS)
    of_out = range(NI * PARTS, NQ)

    def halo(step):
        cur = u_ref if step == 0 else snaps.at[step]
        faces = [
            (cur.at[pl.ds(rows - CY, CY)], hx.at[step, 0], sides[0][0]),
            (cur.at[pl.ds(0, CY)], hx.at[step, 1], sides[0][1]),
            (hy_out.at[step, 0], hy.at[step, 0], sides[1][0]),
            (hy_out.at[step, 1], hy.at[step, 1], sides[1][1]),
            (hz_out.at[step, 0], hz.at[step, 0], sides[2][0]),
            (hz_out.at[step, 1], hz.at[step, 1], sides[2][1]),
        ]
        return [
            remote(s, d, halo_s.at[step, i], halo_r.at[step, i], dev)
            for i, (s, d, dev) in enumerate(faces)
        ]

    lane = lax.broadcasted_iota(jnp.int32, (CY, 128), 1)

    def halo_x(step):
        copies = halo(step)
        for side, i in enumerate((CX - 1, 0)):
            copies[side].start()

    def halo_yz(step):
        copies = halo(step)
        lo = jnp.zeros((CY, 128), F32)
        hi = jnp.zeros((CY, 128), F32)
        for i in range(CX):
            hy_out[step, 0, pl.ds(i, 1), :] = snaps[step, pl.ds(i * CY + CY - 1, 1), :]
            hy_out[step, 1, pl.ds(i, 1), :] = snaps[step, pl.ds(i * CY, 1), :]
            last = snaps[step, pl.ds(i * CY, CY), pl.ds(PEN - 128, 128)]
            head = snaps[step, pl.ds(i * CY, CY), pl.ds(0, 128)]
            hi = jnp.where(lane == i, pltpu.roll(last, i + 1, 1), hi)
            lo = jnp.where(lane == i, pltpu.roll(head, i, 1) if i else head, lo)
        hz_out[step, 0] = hi
        hz_out[step, 1] = lo
        for c in copies[2:]:
            c.start()

    row_id = lax.broadcasted_iota(jnp.int32, (CY, PEN), 0)
    lane_id = lax.broadcasted_iota(jnp.int32, (CY, PEN), 1)

    def layer(step, i):
        if i < 0:
            return hx[step, 0]
        if i >= CX:
            return hx[step, 1]
        return snaps[step, pl.ds(i * CY, CY), :]

    def advance(step, i):
        u = layer(step, i)
        xp, xm = layer(step, i + 1), layer(step, i - 1)
        yp = jnp.where(row_id == CY - 1, hy[step, 1, pl.ds(i, 1), :], pltpu.roll(u, CY - 1, 0))
        ym = jnp.where(row_id == 0, hy[step, 0, pl.ds(i, 1), :], pltpu.roll(u, 1, 0))
        zhi = hz[step, 1][:, i:i + 1]
        zlo = hz[step, 0][:, i:i + 1]
        zp = jnp.where(lane_id == PEN - 1, zhi, pltpu.roll(u, PEN - 1, 1))
        zm = jnp.where(lane_id == 0, zlo, pltpu.roll(u, 1, 1))
        lap = (xp + xm) + (yp + ym) + (zp + zm) - 6.0 * u
        adv = vel[0, i] * (xp - xm) + vel[1, i] * (yp - ym) + vel[2, i] * (zp - zm)
        new = u + TIME_STEP * (lap - 0.5 * adv - rate[i] * u)
        snaps[step + 1, pl.ds(i * CY, CY), :] = new

    def inner(step):
        for c in halo(step)[2:]:
            c.wait_recv()
        for i in range(1, CX - 1):
            advance(step, i)

    def outer(step):
        for c in halo(step)[:2]:
            c.wait_recv()
        for i in sorted({0, CX - 1}):
            advance(step, i)

    def x_copy(n, k):
        to, _, src = e_pairs[k]
        cols = pl.ds(n * PEN, PEN)
        sems = (x_s.at[n, k], x_r.at[n, k])
        mine, other = xin.at[me_e, :, cols], xin.at[src, :, cols]
        return remote(mine, mine, *sems, to), remote(other, other, *sems, to)

    def pick(n):
        xin[me_e, :, pl.ds(n * PEN, PEN)] = mm(hot_t[...], snaps[n + 1].astype(BF16)).astype(BF16)

    def send_picked(n):
        for k in range(NP):
            x_copy(n, k)[0].start()

    def x_wait(n):
        for k in range(NP):
            x_copy(n, k)[1].wait_recv()

    halo_x(0)
    for n in range(FIRST):
        w_start(n, 0)
    load_u.wait()
    halo_yz(0)
    hot = jnp.where(
        lax.broadcasted_iota(jnp.int32, (rows, S), 0) == picks_ref[...], 1.0, 0.0
    )
    hot_t[...] = jnp.transpose(hot).astype(BF16)
    load_v.wait()
    load_r.wait()
    inner(0)
    outer(0)
    halo_x(1)
    halo_yz(1)
    pick(0)
    if EARLY:
        send_picked(0)
    for n in range(FIRST, SECOND):
        w_start(n, 0)
    for n in of_in0:
        w_next(n, 1)
    inner(1)
    outer(1)
    if not EARLY:
        send_picked(0)
    pick(1)
    send_picked(1)
    for n in range(SECOND, NQ):
        w_start(n, 0)
    for n in of_in1:
        w_next(n, 1)
    w_inner(of_in0)
    for n in of_out:
        w_next(n, 1)
    halo_x(2)
    halo_yz(2)
    w_inner(of_in1)
    w_last(of_in0)

    SA = NE * S
    PH = PEN // PARTS
    cb = 4 if NW % 4 == 0 else NW
    HB = cb * Hc
    NB = NW // cb

    def weight(m, b):
        return wts[m, pl.ds(b * cb, cb)].reshape(HB, PEN)

    def x_half(n):
        return xin[:, :, pl.ds(n * PEN, PEN)].reshape(SA, PEN)

    x_wait(0)
    for b in range(NB):
        pre[pl.ds(b * cb, cb)] = mm(weight(0, b), x_half(0), NT).reshape(cb, Hc, SA)
    w_inner(of_out)
    w_last(of_in1)

    def part_cols(h):
        return pl.ds(h * PH, PH)

    def p_copies(h, k):
        to = e_pairs[k][0]
        return (
            remote(p_out.at[h, k], p_in.at[h, k], p_s.at[0, h, k], p_r.at[0, h, k], to),
            remote(p_unit_out.at[h, k], p_unit_in.at[h, k], p_s.at[1, h, k], p_r.at[1, h, k], to),
        )

    x_wait(1)
    for b in range(NB):
        blk = pl.ds(b * cb, cb)
        v = pre[blk].reshape(HB, SA) + mm(weight(1, b), x_half(1), NT)
        pre[blk] = v.reshape(cb, Hc, SA)
        hid[blk] = (v / (1.0 + jnp.exp(-v))).astype(BF16).reshape(cb, Hc, SA)
    for h in range(PARTS):
        w_last(of_out[h:h + 1])
        pf[:, :, part_cols(h)] = mm(
            hid[...].reshape(NW * Hc, SA), wts[NI, :, :, part_cols(h)].reshape(NW * Hc, PH), TN
        ).reshape(NE, S, PH)
        for k in range(NP):
            q, unit = encode(pf[e_pairs[k][1], :, part_cols(h)])
            p_out[h, k] = q
            p_unit_out[h, k] = unit
            for c in p_copies(h, k):
                c.start()

    inner(2)
    outer(2)
    snap3 = snaps[STEPS]
    adv_ref[...] = snap3.reshape(CX, CY, PEN)
    hi = snap3.astype(BF16)
    rest = snap3 - hi.astype(F32)
    mid = rest.astype(BF16)
    low = (rest - mid.astype(F32)).astype(BF16)
    ht = hot_t[...]
    tgt[...] = (mm(ht, hi) + mm(ht, mid)) + mm(ht, low)

    def r_copy(h, k):
        to, _, src = e_pairs[k]
        sems = (r_s.at[h, k], r_r.at[h, k])
        mine, other = res.at[h, me_e], res.at[h, src]
        return remote(mine, mine, *sems, to), remote(other, other, *sems, to)

    for h in range(PARTS):
        total = pf[me_e, :, part_cols(h)] - tgt[:, part_cols(h)]
        for k in range(NP):
            for c in p_copies(h, k):
                c.wait_recv()
            total = total + decode(p_in[h, k], p_unit_in[h, k])
        res[h, me_e] = (total * scale).astype(BF16)
        for k in range(NP):
            r_copy(h, k)[0].start()

    for b in range(NB):
        blk = pl.ds(b * cb, cb)
        v = pre[blk]
        sig = 1.0 / (1.0 + jnp.exp(-v))
        pre[blk] = sig * (1.0 + v * (1.0 - sig))

    starts = [sum(widths[:c]) for c in range(len(widths))]

    def cols_of(c):
        return pl.ds(starts[c], widths[c])

    def q_rows(stage):
        return sum((NW >> (s + 1)) for s in range(1, stage))

    def core_copy(c):
        half = NW // 2
        return remote(
            g.at[pl.ds((1 - mb[0]) * half, half), :, cols_of(c)], core_in.at[:, :, cols_of(c)],
            g_s.at[0, 0, c], g_r.at[0, 0, c], w_partner(0),
        )

    def stage_copies(c, stage):
        size = NW >> (stage + 1)
        blk = pl.ds(q_rows(stage), size)
        one = pl.ds(stage - 1, 1)
        return (
            remote(q_out.at[blk, :, cols_of(c)], q_in.at[blk, :, cols_of(c)],
                   g_s.at[stage, 0, c], g_r.at[stage, 0, c], w_partner(stage)),
            remote(u_out.at[one, :, cols_of(c)], u_in.at[one, :, cols_of(c)],
                   g_s.at[stage, 1, c], g_r.at[stage, 1, c], w_partner(stage)),
        )

    def base_of(stage):
        return sum(mb[j] * (1 << (nw - 1 - j)) for j in range(stage))

    def put(c, val):
        g[:, :, cols_of(c)] = val.reshape(NW, Hc, widths[c])
        core_copy(c).start()

    def reduce(c, stage):
        size = NW >> (stage + 1)
        W = widths[c]
        flat = size * Hc
        if stage == 0:
            core_copy(c).wait_recv()

            def came(off, n):
                return core_in[pl.ds(off, n), :, cols_of(c)].reshape(n * Hc, W)
        else:
            for cp in stage_copies(c, stage):
                cp.wait_recv()
            unit = u_in[stage - 1, :, cols_of(c)]

            def came(off, n):
                return decode(q_in[pl.ds(q_rows(stage) + off, n), :, cols_of(c)].reshape(n * Hc, W), unit)
        base = base_of(stage + 1)
        if size == 1:
            val = g[base, :, cols_of(c)] + came(0, 1)
            if starts[c] < PEN:
                gout_ref[:, cols_of(c)] = val
            else:
                gin_ref[:, pl.ds(starts[c] - PEN, W)] = val
            return
        half = size // 2
        nxt = mb[stage + 1]
        away, keep = (1 - nxt) * half, nxt * half
        val = g[pl.ds(base + away, half), :, cols_of(c)].reshape(half * Hc, W) + came(away, half)
        q, unit_out = encode(val)
        q_out[pl.ds(q_rows(stage + 1), half), :, cols_of(c)] = q.reshape(half, Hc, W)
        u_out[stage, :, cols_of(c)] = unit_out
        for cp in stage_copies(c, stage + 1):
            cp.start()
        val = g[pl.ds(base + keep, half), :, cols_of(c)].reshape(half * Hc, W) + came(keep, half)
        g[pl.ds(base + keep, half), :, cols_of(c)] = val.reshape(half, Hc, W)

    C = len(widths)
    first = [c for c in range(C) if starts[c] < PEN]
    reduced = 0
    for h in range(PARTS):
        for k in range(NP):
            r_copy(h, k)[1].wait_recv()
        for c in first:
            if starts[c] // PH == h:
                r = res[h, :, :, pl.ds(starts[c] - h * PH, widths[c])].reshape(SA, widths[c])
                put(c, mm(hid[...].reshape(NW * Hc, SA), r))
        if h < PARTS - 1:
            while reduced < len(first) and starts[reduced] // PH == h:
                reduce(reduced, 0)
                reduced += 1
    for b in range(NB):
        blk = pl.ds(b * cb, cb)
        back = sum(
            mm(wts[NI, blk, :, part_cols(h)].reshape(HB, PH), res[h].reshape(SA, PH), NT)
            for h in range(PARTS)
        )
        hid[blk] = (back * pre[blk].reshape(HB, SA)).astype(BF16).reshape(cb, Hc, SA)
        while b == 0 and reduced < len(first):
            reduce(reduced, 0)
            reduced += 1
    for c in range(len(first), C):
        x = xin[:, :, pl.ds(starts[c] - PEN, widths[c])].reshape(SA, widths[c])
        put(c, mm(hid[...].reshape(NW * Hc, SA), x))
        if reduced < c - 1:
            reduce(reduced, 0)
            reduced += 1
    while reduced < C:
        reduce(reduced, 0)
        reduced += 1
    lag = 2
    for t in range(C + lag * nw):
        for stage in range(1, nw):
            c = t - lag * (stage - 1)
            if 0 <= c < C:
                reduce(c, stage)

    for step in range(STEPS):
        for cp in halo(step):
            cp.wait_send()
    for n in range(NQ):
        if nw == 1 and n % PARTS == 0:
            load_w[n // PARTS].wait()
        for stage in range(nw):
            w_copy(n, stage)[0].wait_send()
    for k in range(NP):
        for n in range(NI):
            x_copy(n, k)[0].wait_send()
        for h in range(PARTS):
            for cp in p_copies(h, k):
                cp.wait_send()
            r_copy(h, k)[0].wait_send()
    for c in range(C):
        core_copy(c).wait_send()
        for stage in range(1, nw):
            for cp in stage_copies(c, stage):
                cp.wait_send()


def finish(*refs):
    n = (len(refs) - 1) // 2
    sems = refs[-1]
    copies = [pltpu.make_async_copy(refs[i], refs[n + i], sems.at[i]) for i in range(n)]
    for c in copies:
        c.start()
    for c in copies:
        c.wait()


def shards(sizes, scalar_field, velocity, reaction_rate, sample_cells, weight_in, weight_out):
    T, NY, NZ = sizes
    NE = NY * 2
    NW = NZ * (T // 2)
    NP = NE - 1
    nw = log2(NW)
    CX, CY, PEN = scalar_field.shape
    S = sample_cells.shape[-1]
    SA = NE * S
    PH = PEN // PARTS
    Hc, IN = weight_in.shape
    NI = IN // PEN
    NM = NI + 1
    wide = IN + PEN
    W = PEN // 2
    widths = (W // 2,) * 2 + (W,) * (wide // W - 2) + (W // 2,) * 2
    C = len(widths)
    scale = 1.0 / math.sqrt(S * T * NY * NZ)
    rows = CX * CY
    dma = pltpu.SemaphoreType.DMA
    vmem = pl.BlockSpec(memory_space=pltpu.VMEM)
    hbm = pl.BlockSpec(memory_space=pltpu.HBM)
    shapes = ((CX, CY, PEN), (Hc, IN), (Hc, PEN))
    outs = (pl.pallas_call(
        functools.partial(kernel, sizes, scale, widths),
        out_shape=tuple(pltpu.VMEM(s, F32) for s in shapes),
        in_specs=[hbm, hbm, hbm, vmem, hbm, hbm],
        out_specs=(vmem,) * 3,
        scratch_shapes=[
            pltpu.VMEM((STEPS + 1, rows, PEN), F32),
            pltpu.VMEM((3, CX, CY, PEN), F32),
            pltpu.VMEM((CX, CY, PEN), F32),
            pltpu.VMEM((STEPS, 2, CY, PEN), F32),
            pltpu.VMEM((STEPS, 2, CX, PEN), F32),
            pltpu.VMEM((STEPS, 2, CX, PEN), F32),
            pltpu.VMEM((STEPS, 2, CY, 128), F32),
            pltpu.VMEM((STEPS, 2, CY, 128), F32),
            pltpu.VMEM((S, rows), BF16),
            pltpu.VMEM((NE, S, IN), BF16),
            pltpu.VMEM((NM, NW, Hc, PEN), BF16),
            pltpu.VMEM((NW, Hc, SA), F32),
            pltpu.VMEM((NW, Hc, SA), BF16),
            pltpu.VMEM((NE, S, PEN), F32),
            pltpu.VMEM((S, PEN), F32),
            pltpu.VMEM((PARTS, NP, S, PH), I16),
            pltpu.VMEM((PARTS, NP, S, PH), I16),
            pltpu.VMEM((PARTS, NP, 1, PH), F32),
            pltpu.VMEM((PARTS, NP, 1, PH), F32),
            pltpu.VMEM((PARTS, NE, S, PH), BF16),
            pltpu.VMEM((NW, Hc, wide), F32),
            pltpu.VMEM((NW // 2, Hc, wide), F32),
            pltpu.VMEM((NW // 2 - 1, Hc, wide), I16),
            pltpu.VMEM((NW // 2 - 1, Hc, wide), I16),
            pltpu.VMEM((nw - 1, 1, wide), F32),
            pltpu.VMEM((nw - 1, 1, wide), F32),
            dma((STEPS, 6)), dma((STEPS, 6)),
            dma((NI, NP)), dma((NI, NP)),
            dma((NM * PARTS, nw)), dma((NM * PARTS, nw)),
            dma((2, PARTS, NP)), dma((2, PARTS, NP)),
            dma((PARTS, NP)), dma((PARTS, NP)),
            dma((nw, 2, C)), dma((nw, 2, C)),
            dma((3 + NM,)),
        ],
        compiler_params=pltpu.CompilerParams(
            collective_id=0, has_side_effects=True, vmem_limit_bytes=56 * 1024 * 1024
        ),
    )(
        scalar_field.reshape(rows, PEN), velocity, reaction_rate,
        sample_cells.reshape(1, S), weight_in, weight_out,
    ))
    outs = tuple(pltpu.with_memory_space_constraint(o, pltpu.VMEM) for o in outs)
    return tuple(pl.pallas_call(
        finish,
        out_shape=tuple(jax.ShapeDtypeStruct(s, F32) for s in shapes),
        in_specs=[vmem] * 3,
        out_specs=(hbm,) * 3,
        scratch_shapes=[dma((3,))],
    )(*outs))


def solution(mesh):
    sizes = (mesh.shape["gx"], mesh.shape["gy"], mesh.shape["gz"])
    in_specs = (
        P("gx", "gy", "gz"),
        P(None, "gx", "gy", "gz"),
        P("gx", "gy", "gz"),
        P("gx", "gy", "gz"),
        P(("gx", "gy", "gz"), None),
        P(("gx", "gy", "gz"), None),
    )
    out_specs = (P("gx", "gy", "gz"), P(("gx", "gy", "gz"), None), P(("gx", "gy", "gz"), None))
    return jax.shard_map(
        functools.partial(shards, sizes), mesh=mesh, in_specs=in_specs, out_specs=out_specs,
        check_vma=False,
    )
```

```python
import functools
import math

import jax
import jax.numpy as jnp
from jax import lax
from jax.experimental import pallas as pl
from jax.experimental.pallas import tpu as pltpu
from jax.sharding import PartitionSpec as P

STEPS = 3
FIRST, SECOND, EARLY = 3, 6, True
TIME_STEP = 0.15
PARTS = 2
LAG = 2
AHEAD = 1
SWAPPED = (0, 3)
RELAYED = 1
NT = (((1,), (1,)), ((), ()))
TN = (((0,), (0,)), ((), ()))
F32 = jnp.float32
BF16 = jnp.bfloat16
I16 = jnp.int16
TOP = 32766.0
TINY = 1e-30


def mm(a, b, dims=None):
    if dims is None:
        return jnp.dot(a, b, preferred_element_type=F32)
    return lax.dot_general(a, b, dims, preferred_element_type=F32)


def log2(n):
    bits = n.bit_length() - 1
    assert 1 << bits == n
    return bits


def encode(x):
    top = jnp.maximum(jnp.max(jnp.abs(x), axis=0, keepdims=True), TINY)
    return jnp.round(x * (TOP / top)).astype(I16), top * (1.0 / TOP)


def encode_all(parts):
    top = TINY
    for x in parts:
        top = jnp.maximum(top, jnp.max(jnp.abs(x), axis=0, keepdims=True))
    by = TOP / top
    return [jnp.round(x * by).astype(I16) for x in parts], top * (1.0 / TOP)


def decode(q, unit):
    return q.astype(F32) * unit


def kernel(
    sizes, scale, widths,
    u_ref, vel_ref, rate_ref, picks_ref, win_ref, wout_ref,
    adv_ref, gin_ref, gout_ref,
    snaps, vel, rate, hx, hx_out, hu, hu_out, hy_out, hy, hz_out, hz, hot_t, xin, wts, pre, hid, pf, tgt,
    p_out, p_in, p_unit_out, p_unit_in, res, g, core_in, q_out, q_in, u_out, u_in,
    halo_s, halo_r, x_s, x_r, w_s, w_r, p_s, p_r, r_s, r_r, g_s, g_r, loc,
):
    T, NY, NZ = sizes
    gx, gy, gz = lax.axis_index("gx"), lax.axis_index("gy"), lax.axis_index("gz")
    CX, CY, PEN = vel.shape[1:]
    rows = CX * CY
    S = hot_t.shape[0]
    Hc, IN = win_ref.shape
    NI = IN // PEN
    NE = NY * 2
    gxh, gxl = gx // 2, gx % 2
    me_e = gy * 2 + gxl
    wbits = [("gz", b) for b in range(log2(NZ))] + [("gx", b) for b in range(1, log2(T))]
    nw = len(wbits)
    NW = 1 << nw
    index = {"gx": gx, "gy": gy, "gz": gz}
    mb = [(index[a] // (1 << b)) % 2 for a, b in wbits]
    me_w = sum(mb[i] * (1 << (nw - 1 - i)) for i in range(nw))

    def w_partner(i):
        a, b = wbits[i]
        return {a: index[a] + (1 - 2 * mb[i]) * (1 << b)}

    e_pairs, straight = [], []
    for dy in range(NY):
        for dx in range(2):
            if dy or dx:
                lo = (gxl + dx) % 2
                to = {"gy": (gy + dy) % NY, "gx": gxh * 2 + lo}
                e_pairs.append((to, ((gy + dy) % NY) * 2 + lo, ((gy + NY - dy) % NY) * 2 + lo))
                straight.append(dy == 0 or dx == 0)
    e_pairs, straight = e_pairs[::-1], straight[::-1]
    NP = NE - 1
    NEAR = NP - 1

    sides = [
        ({"gx": (gx + 1) % T}, {"gx": (gx + T - 1) % T}),
        ({"gy": (gy + 1) % NY}, {"gy": (gy + NY - 1) % NY}),
        ({"gz": (gz + 1) % NZ}, {"gz": (gz + NZ - 1) % NZ}),
    ]

    def remote(src, dst, ss, rs, dev):
        return pltpu.make_async_remote_copy(
            src_ref=src, dst_ref=dst, send_sem=ss, recv_sem=rs,
            device_id=dev, device_id_type=pl.DeviceIdType.MESH,
        )

    load_u = pltpu.make_async_copy(u_ref, snaps.at[0], loc.at[0])
    load_v = pltpu.make_async_copy(vel_ref, vel, loc.at[1])
    load_r = pltpu.make_async_copy(rate_ref, rate, loc.at[2])
    NM = NI + 1
    sources = [win_ref.at[:, pl.ds(i * PEN, PEN)] for i in range(NI)] + [wout_ref]
    load_w = [pltpu.make_async_copy(sources[i], wts.at[i, me_w], loc.at[3 + i]) for i in range(NM)]
    load_u.start()
    load_v.start()
    load_r.start()
    for c in load_w:
        c.start()

    barrier = pltpu.get_barrier_semaphore()
    greet = [p[0] for p in e_pairs] + [w_partner(i) for i in range(nw)]
    for pair in sides:
        greet += list(pair)
    for dev in greet:
        pl.semaphore_signal(barrier, inc=1, device_id=dev, device_id_type=pl.DeviceIdType.MESH)
    pl.semaphore_wait(barrier, len(greet))

    WP = PEN // PARTS
    pieces = [(m, part) for m in range(NM) for part in range(PARTS)]

    def w_copy(n, stage):
        m, part = pieces[n]
        cols = pl.ds(part * WP, WP)
        i = nw - 1 - stage
        size = 1 << stage
        base = sum(mb[j] * (1 << (nw - 1 - j)) for j in range(i + 1))
        theirs = base + (1 - 2 * mb[i]) * size
        sems = (w_s.at[n, stage], w_r.at[n, stage])
        if stage == 0:
            src = win_ref.at[:, pl.ds(m * PEN + part * WP, WP)] if m < NI else wout_ref.at[:, cols]
            send = remote(src, wts.at[m, me_w, :, cols], *sems, w_partner(i))
        else:
            mine = wts.at[m, pl.ds(base, size), :, cols]
            send = remote(mine, mine, *sems, w_partner(i))
        other = wts.at[m, pl.ds(theirs, size), :, cols]
        recv = remote(other, other, *sems, w_partner(i))
        return send, recv

    def w_start(n, stage):
        if stage == 1 and n % PARTS == 0:
            load_w[n // PARTS].wait()
        w_copy(n, stage)[0].start()

    def w_next(n, stage):
        w_copy(n, stage - 1)[1].wait_recv()
        if stage < nw:
            w_start(n, stage)

    def w_inner(group):
        for n in group:
            for stage in range(2, nw):
                w_next(n, stage)

    def w_last(group):
        if nw > 1:
            for n in group:
                w_next(n, nw)

    NQ = len(pieces)
    of_in0 = range(PARTS)
    of_in1 = range(PARTS, NI * PARTS)
    of_out = range(NI * PARTS, NQ)

    def halo(step):
        faces = [
            (hx_out.at[step, 0], hx.at[step, 0], sides[0][0]),
            (hx_out.at[step, 1], hx.at[step, 1], sides[0][1]),
            (hu_out.at[step, 0], hu.at[step, 0], sides[0][0]),
            (hu_out.at[step, 1], hu.at[step, 1], sides[0][1]),
            (hy_out.at[step, 0], hy.at[step, 0], sides[1][0]),
            (hy_out.at[step, 1], hy.at[step, 1], sides[1][1]),
            (hz_out.at[step, 0], hz.at[step, 0], sides[2][0]),
            (hz_out.at[step, 1], hz.at[step, 1], sides[2][1]),
        ]
        return [
            remote(s, d, halo_s.at[step, i], halo_r.at[step, i], dev)
            for i, (s, d, dev) in enumerate(faces)
        ]

    lane = lax.broadcasted_iota(jnp.int32, (CY, 128), 1)

    def halo_x(step):
        copies = halo(step)
        for side, i in enumerate((CX - 1, 0)):
            q, unit = encode(snaps[step, pl.ds(i * CY, CY), :])
            hx_out[step, side] = q
            hu_out[step, side] = unit
            copies[side].start()
            copies[2 + side].start()

    def halo_yz(step):
        copies = halo(step)
        lo = jnp.zeros((CY, 128), F32)
        hi = jnp.zeros((CY, 128), F32)
        for i in range(CX):
            hy_out[step, 0, pl.ds(i, 1), :] = snaps[step, pl.ds(i * CY + CY - 1, 1), :]
            hy_out[step, 1, pl.ds(i, 1), :] = snaps[step, pl.ds(i * CY, 1), :]
            last = snaps[step, pl.ds(i * CY, CY), pl.ds(PEN - 128, 128)]
            head = snaps[step, pl.ds(i * CY, CY), pl.ds(0, 128)]
            hi = jnp.where(lane == i, pltpu.roll(last, i + 1, 1), hi)
            lo = jnp.where(lane == i, pltpu.roll(head, i, 1) if i else head, lo)
        hz_out[step, 0] = hi
        hz_out[step, 1] = lo
        for c in copies[4:]:
            c.start()

    row_id = lax.broadcasted_iota(jnp.int32, (CY, PEN), 0)
    lane_id = lax.broadcasted_iota(jnp.int32, (CY, PEN), 1)

    def layer(step, i):
        if i < 0:
            return decode(hx[step, 0], hu[step, 0])
        if i >= CX:
            return decode(hx[step, 1], hu[step, 1])
        return snaps[step, pl.ds(i * CY, CY), :]

    def advance(step, i):
        u = layer(step, i)
        xp, xm = layer(step, i + 1), layer(step, i - 1)
        yp = jnp.where(row_id == CY - 1, hy[step, 1, pl.ds(i, 1), :], pltpu.roll(u, CY - 1, 0))
        ym = jnp.where(row_id == 0, hy[step, 0, pl.ds(i, 1), :], pltpu.roll(u, 1, 0))
        zhi = hz[step, 1][:, i:i + 1]
        zlo = hz[step, 0][:, i:i + 1]
        zp = jnp.where(lane_id == PEN - 1, zhi, pltpu.roll(u, PEN - 1, 1))
        zm = jnp.where(lane_id == 0, zlo, pltpu.roll(u, 1, 1))
        lap = (xp + xm) + (yp + ym) + (zp + zm) - 6.0 * u
        adv = vel[0, i] * (xp - xm) + vel[1, i] * (yp - ym) + vel[2, i] * (zp - zm)
        new = u + TIME_STEP * (lap - 0.5 * adv - rate[i] * u)
        snaps[step + 1, pl.ds(i * CY, CY), :] = new

    def inner(step):
        for c in halo(step)[4:]:
            c.wait_recv()
        for i in range(1, CX - 1):
            advance(step, i)

    def outer(step):
        for c in halo(step)[:4]:
            c.wait_recv()
        for i in sorted({0, CX - 1}):
            advance(step, i)

    def x_copy(n, k):
        to, _, src = e_pairs[k]
        cols = pl.ds(n * PEN, PEN)
        sems = (x_s.at[n, k], x_r.at[n, k])
        own = me_e
        if n < RELAYED and not straight[k]:
            to, own = {"gy": to["gy"]}, gy * 2 + (1 - gxl)
        mine, other = xin.at[own, :, cols], xin.at[src, :, cols]
        return remote(mine, mine, *sems, to), remote(other, other, *sems, to)

    def pick(n):
        xin[me_e, :, pl.ds(n * PEN, PEN)] = mm(hot_t[...], snaps[n + 1].astype(BF16)).astype(BF16)

    def send_picked(n):
        for k in range(NP):
            if n >= RELAYED or straight[k]:
                x_copy(n, k)[0].start()

    def x_forward(n):
        if n < RELAYED:
            x_copy(n, NEAR)[1].wait_recv()
            for k in range(NP):
                if not straight[k]:
                    x_copy(n, k)[0].start()

    def x_wait(n):
        for k in range(NP):
            if n >= RELAYED or k != NEAR:
                x_copy(n, k)[1].wait_recv()

    load_u.wait()
    halo_x(0)
    for n in range(FIRST):
        w_start(n, 0)
    halo_yz(0)
    hot = jnp.where(
        lax.broadcasted_iota(jnp.int32, (rows, S), 0) == picks_ref[...], 1.0, 0.0
    )
    hot_t[...] = jnp.transpose(hot).astype(BF16)
    load_v.wait()
    load_r.wait()
    inner(0)
    outer(0)
    halo_x(1)
    halo_yz(1)
    pick(0)
    if EARLY:
        send_picked(0)
    for n in range(FIRST, SECOND):
        w_start(n, 0)
    for n in of_in0:
        w_next(n, 1)
    inner(1)
    outer(1)
    if not EARLY:
        send_picked(0)
    pick(1)
    send_picked(1)
    x_forward(0)
    for n in range(SECOND, NQ):
        w_start(n, 0)
    for n in of_in1:
        w_next(n, 1)
    w_inner(of_in0)
    for n in of_out:
        w_next(n, 1)
    halo_x(2)
    halo_yz(2)
    w_inner(of_in1)
    x_forward(1)
    w_last(of_in0)

    SA = NE * S
    PH = PEN // PARTS
    cb = 4 if NW % 4 == 0 else NW
    HB = cb * Hc
    NB = NW // cb

    def weight(m, b):
        return wts[m, pl.ds(b * cb, cb)].reshape(HB, PEN)

    def x_half(n):
        return xin[:, :, pl.ds(n * PEN, PEN)].reshape(SA, PEN)

    x_wait(0)
    for b in range(NB):
        pre[pl.ds(b * cb, cb)] = mm(weight(0, b), x_half(0), NT).reshape(cb, Hc, SA)
    w_inner(of_out)
    w_last(of_in1)

    def part_cols(h):
        return pl.ds(h * PH, PH)

    def p_copies(h, k):
        to = e_pairs[k][0]
        return (
            remote(p_out.at[h, k], p_in.at[h, k], p_s.at[0, h, k], p_r.at[0, h, k], to),
            remote(p_unit_out.at[h, k], p_unit_in.at[h, k], p_s.at[1, h, k], p_r.at[1, h, k], to),
        )

    x_wait(1)
    for b in range(NB):
        blk = pl.ds(b * cb, cb)
        v = pre[blk].reshape(HB, SA) + mm(weight(1, b), x_half(1), NT)
        pre[blk] = v.reshape(cb, Hc, SA)
        hid[blk] = (v / (1.0 + jnp.exp(-v))).astype(BF16).reshape(cb, Hc, SA)
    for h in range(PARTS):
        w_last(of_out[h:h + 1])
        pf[:, :, part_cols(h)] = mm(
            hid[...].reshape(NW * Hc, SA), wts[NI, :, :, part_cols(h)].reshape(NW * Hc, PH), TN
        ).reshape(NE, S, PH)
        for k in range(NP):
            q, unit = encode(pf[e_pairs[k][1], :, part_cols(h)])
            p_out[h, k] = q
            p_unit_out[h, k] = unit
            for c in p_copies(h, k):
                c.start()

    inner(2)
    outer(2)
    snap3 = snaps[STEPS]
    adv_ref[...] = snap3.reshape(CX, CY, PEN)
    hi = snap3.astype(BF16)
    rest = snap3 - hi.astype(F32)
    mid = rest.astype(BF16)
    low = (rest - mid.astype(F32)).astype(BF16)
    ht = hot_t[...]
    tgt[...] = (mm(ht, hi) + mm(ht, mid)) + mm(ht, low)

    def r_copy(h, k):
        to, _, src = e_pairs[k]
        sems = (r_s.at[h, k], r_r.at[h, k])
        mine, other = res.at[h, me_e], res.at[h, src]
        return remote(mine, mine, *sems, to), remote(other, other, *sems, to)

    for h in range(PARTS):
        total = pf[me_e, :, part_cols(h)] - tgt[:, part_cols(h)]
        for k in range(NP):
            for c in p_copies(h, k):
                c.wait_recv()
            total = total + decode(p_in[h, k], p_unit_in[h, k])
        res[h, me_e] = (total * scale).astype(BF16)
        for k in range(NP):
            r_copy(h, k)[0].start()

    for b in range(NB):
        blk = pl.ds(b * cb, cb)
        v = pre[blk]
        sig = 1.0 / (1.0 + jnp.exp(-v))
        pre[blk] = sig * (1.0 + v * (1.0 - sig))

    starts = [sum(widths[:c]) for c in range(len(widths))]

    def cols_of(c):
        return pl.ds(starts[c], widths[c])

    def q_rows(stage):
        return sum((NW >> (s + 1)) for s in range(1, stage))

    def core_copy(c):
        half = NW // 2
        return remote(
            g.at[pl.ds((1 - mb[0]) * half, half), :, cols_of(c)], core_in.at[:, :, cols_of(c)],
            g_s.at[0, 0, c], g_r.at[0, 0, c], w_partner(0),
        )

    def bit(i):
        return 1 << (nw - 1 - i)

    orders = [
        [0] + (list(range(nw - 1, 0, -1)) if c in SWAPPED else list(range(1, nw)))
        for c in range(len(widths))
    ]

    def stage_copies(c, stage):
        size = NW >> (stage + 1)
        blk = pl.ds(q_rows(stage), size)
        one = pl.ds(stage - 1, 1)
        to = w_partner(orders[c][stage])
        return (
            remote(q_out.at[blk, :, cols_of(c)], q_in.at[blk, :, cols_of(c)],
                   g_s.at[stage, 0, c], g_r.at[stage, 0, c], to),
            remote(u_out.at[one, :, cols_of(c)], u_in.at[one, :, cols_of(c)],
                   g_s.at[stage, 1, c], g_r.at[stage, 1, c], to),
        )

    def put(c, val):
        g[:, :, cols_of(c)] = val.reshape(NW, Hc, widths[c])
        core_copy(c).start()

    def reduce(c, stage):
        cols = cols_of(c)
        order = orders[c]
        rest = order[stage + 1:]
        base = sum(mb[i] * bit(i) for i in order[:stage + 1])
        if stage == 0:
            core_copy(c).wait_recv()
        else:
            for cp in stage_copies(c, stage):
                cp.wait_recv()
            unit = u_in[stage - 1, :, cols]

        def added(vals):
            place = sum(v * bit(i) for v, i in zip(vals, rest))
            if stage == 0:
                came = core_in[place, :, cols]
            else:
                slot = q_rows(stage) + sum(v * (1 << (len(rest) - 1 - t)) for t, v in enumerate(vals))
                came = decode(q_in[slot, :, cols], unit)
            return base + place, g[base + place, :, cols] + came

        if not rest:
            val = added([])[1]
            if starts[c] < PEN:
                gout_ref[:, cols] = val
            else:
                gin_ref[:, pl.ds(starts[c] - PEN, widths[c])] = val
            return
        nxt = mb[rest[0]]
        n = len(rest) - 1
        tails = [[(k >> (n - 1 - t)) & 1 for t in range(n)] for k in range(1 << n)]
        away = [added([1 - nxt] + tail)[1] for tail in tails]
        codes, unit_out = encode_all(away)
        for k, q in enumerate(codes):
            q_out[q_rows(stage + 1) + k, :, cols] = q
        u_out[stage, :, cols] = unit_out
        for cp in stage_copies(c, stage + 1):
            cp.start()
        for tail in tails:
            place, val = added([nxt] + tail)
            g[place, :, cols] = val

    C = len(widths)
    first = [c for c in range(C) if starts[c] < PEN]
    reduced = 0
    for h in range(PARTS):
        for k in range(NP):
            r_copy(h, k)[1].wait_recv()
        for c in first:
            if starts[c] // PH == h:
                r = res[h, :, :, pl.ds(starts[c] - h * PH, widths[c])].reshape(SA, widths[c])
                put(c, mm(hid[...].reshape(NW * Hc, SA), r))
        if h < PARTS - 1:
            while reduced < len(first) and starts[reduced] // PH == h:
                reduce(reduced, 0)
                reduced += 1
    for b in range(NB):
        blk = pl.ds(b * cb, cb)
        back = sum(
            mm(wts[NI, blk, :, part_cols(h)].reshape(HB, PH), res[h].reshape(SA, PH), NT)
            for h in range(PARTS)
        )
        hid[blk] = (back * pre[blk].reshape(HB, SA)).astype(BF16).reshape(cb, Hc, SA)
        while b == 0 and reduced < len(first):
            reduce(reduced, 0)
            reduced += 1
    seconds = 0
    for c in range(len(first), C):
        x = xin[:, :, pl.ds(starts[c] - PEN, widths[c])].reshape(SA, widths[c])
        put(c, mm(hid[...].reshape(NW * Hc, SA), x))
        if reduced < c:
            reduce(reduced, 0)
            reduced += 1
        if nw > 1 and AHEAD <= c - len(first) and seconds < len(first) - 1:
            reduce(seconds, 1)
            seconds += 1
    while reduced < C:
        reduce(reduced, 0)
        reduced += 1
    for t in range(C + LAG * nw):
        for stage in range(1, nw):
            c = t - LAG * (stage - 1)
            if 0 <= c < C and (stage > 1 or c >= seconds):
                reduce(c, stage)

    for step in range(STEPS):
        for cp in halo(step):
            cp.wait_send()
    for n in range(NQ):
        if nw == 1 and n % PARTS == 0:
            load_w[n // PARTS].wait()
        for stage in range(nw):
            w_copy(n, stage)[0].wait_send()
    for k in range(NP):
        for n in range(NI):
            x_copy(n, k)[0].wait_send()
        for h in range(PARTS):
            for cp in p_copies(h, k):
                cp.wait_send()
            r_copy(h, k)[0].wait_send()
    for c in range(C):
        core_copy(c).wait_send()
        for stage in range(1, nw):
            for cp in stage_copies(c, stage):
                cp.wait_send()


def finish(*refs):
    n = (len(refs) - 1) // 2
    sems = refs[-1]
    copies = [pltpu.make_async_copy(refs[i], refs[n + i], sems.at[i]) for i in range(n)]
    for c in copies:
        c.start()
    for c in copies:
        c.wait()


def shards(sizes, scalar_field, velocity, reaction_rate, sample_cells, weight_in, weight_out):
    T, NY, NZ = sizes
    NE = NY * 2
    NW = NZ * (T // 2)
    NP = NE - 1
    nw = log2(NW)
    CX, CY, PEN = scalar_field.shape
    S = sample_cells.shape[-1]
    SA = NE * S
    PH = PEN // PARTS
    Hc, IN = weight_in.shape
    NI = IN // PEN
    NM = NI + 1
    wide = IN + PEN
    W = PEN // 2
    widths = (W // 2,) * 2 + (W,) * (wide // W - 2) + (W // 2,) * 2
    C = len(widths)
    scale = 1.0 / math.sqrt(S * T * NY * NZ)
    rows = CX * CY
    dma = pltpu.SemaphoreType.DMA
    vmem = pl.BlockSpec(memory_space=pltpu.VMEM)
    hbm = pl.BlockSpec(memory_space=pltpu.HBM)
    shapes = ((CX, CY, PEN), (Hc, IN), (Hc, PEN))
    outs = (pl.pallas_call(
        functools.partial(kernel, sizes, scale, widths),
        out_shape=tuple(pltpu.VMEM(s, F32) for s in shapes),
        in_specs=[hbm, hbm, hbm, vmem, hbm, hbm],
        out_specs=(vmem,) * 3,
        scratch_shapes=[
            pltpu.VMEM((STEPS + 1, rows, PEN), F32),
            pltpu.VMEM((3, CX, CY, PEN), F32),
            pltpu.VMEM((CX, CY, PEN), F32),
            pltpu.VMEM((STEPS, 2, CY, PEN), I16),
            pltpu.VMEM((STEPS, 2, CY, PEN), I16),
            pltpu.VMEM((STEPS, 2, 1, PEN), F32),
            pltpu.VMEM((STEPS, 2, 1, PEN), F32),
            pltpu.VMEM((STEPS, 2, CX, PEN), F32),
            pltpu.VMEM((STEPS, 2, CX, PEN), F32),
            pltpu.VMEM((STEPS, 2, CY, 128), F32),
            pltpu.VMEM((STEPS, 2, CY, 128), F32),
            pltpu.VMEM((S, rows), BF16),
            pltpu.VMEM((NE, S, IN), BF16),
            pltpu.VMEM((NM, NW, Hc, PEN), BF16),
            pltpu.VMEM((NW, Hc, SA), F32),
            pltpu.VMEM((NW, Hc, SA), BF16),
            pltpu.VMEM((NE, S, PEN), F32),
            pltpu.VMEM((S, PEN), F32),
            pltpu.VMEM((PARTS, NP, S, PH), I16),
            pltpu.VMEM((PARTS, NP, S, PH), I16),
            pltpu.VMEM((PARTS, NP, 1, PH), F32),
            pltpu.VMEM((PARTS, NP, 1, PH), F32),
            pltpu.VMEM((PARTS, NE, S, PH), BF16),
            pltpu.VMEM((NW, Hc, wide), F32),
            pltpu.VMEM((NW // 2, Hc, wide), F32),
            pltpu.VMEM((NW // 2 - 1, Hc, wide), I16),
            pltpu.VMEM((NW // 2 - 1, Hc, wide), I16),
            pltpu.VMEM((nw - 1, 1, wide), F32),
            pltpu.VMEM((nw - 1, 1, wide), F32),
            dma((STEPS, 8)), dma((STEPS, 8)),
            dma((NI, NP)), dma((NI, NP)),
            dma((NM * PARTS, nw)), dma((NM * PARTS, nw)),
            dma((2, PARTS, NP)), dma((2, PARTS, NP)),
            dma((PARTS, NP)), dma((PARTS, NP)),
            dma((nw, 2, C)), dma((nw, 2, C)),
            dma((3 + NM,)),
        ],
        compiler_params=pltpu.CompilerParams(
            collective_id=0, has_side_effects=True, vmem_limit_bytes=56 * 1024 * 1024
        ),
    )(
        scalar_field.reshape(rows, PEN), velocity, reaction_rate,
        sample_cells.reshape(1, S), weight_in, weight_out,
    ))
    outs = tuple(pltpu.with_memory_space_constraint(o, pltpu.VMEM) for o in outs)
    return tuple(pl.pallas_call(
        finish,
        out_shape=tuple(jax.ShapeDtypeStruct(s, F32) for s in shapes),
        in_specs=[vmem] * 3,
        out_specs=(hbm,) * 3,
        scratch_shapes=[dma((3,))],
    )(*outs))


def solution(mesh):
    sizes = (mesh.shape["gx"], mesh.shape["gy"], mesh.shape["gz"])
    in_specs = (
        P("gx", "gy", "gz"),
        P(None, "gx", "gy", "gz"),
        P("gx", "gy", "gz"),
        P("gx", "gy", "gz"),
        P(("gx", "gy", "gz"), None),
        P(("gx", "gy", "gz"), None),
    )
    out_specs = (P("gx", "gy", "gz"), P(("gx", "gy", "gz"), None), P(("gx", "gy", "gz"), None))
    return jax.shard_map(
        functools.partial(shards, sizes), mesh=mesh, in_specs=in_specs, out_specs=out_specs,
        check_vma=False,
    )
```

```python
import functools
import math

import jax
import jax.numpy as jnp
from jax import lax
from jax.experimental import pallas as pl
from jax.experimental.pallas import tpu as pltpu
from jax.sharding import PartitionSpec as P

STEPS = 3
FIRST, SECOND, EARLY = 3, 6, True
TIME_STEP = 0.15
PARTS = 2
LAG = 2
AHEAD = 2
SWAPPED = ()
RELAYED = 1
NT = (((1,), (1,)), ((), ()))
TN = (((0,), (0,)), ((), ()))
F32 = jnp.float32
BF16 = jnp.bfloat16
I16 = jnp.int16
TOP = 32766.0
TINY = 1e-30


def mm(a, b, dims=None):
    if dims is None:
        return jnp.dot(a, b, preferred_element_type=F32)
    return lax.dot_general(a, b, dims, preferred_element_type=F32)


def log2(n):
    bits = n.bit_length() - 1
    assert 1 << bits == n
    return bits


def encode(x):
    top = jnp.maximum(jnp.max(jnp.abs(x), axis=0, keepdims=True), TINY)
    return jnp.round(x * (TOP / top)).astype(I16), top * (1.0 / TOP)


def encode_all(parts):
    top = TINY
    for x in parts:
        top = jnp.maximum(top, jnp.max(jnp.abs(x), axis=0, keepdims=True))
    by = TOP / top
    return [jnp.round(x * by).astype(I16) for x in parts], top * (1.0 / TOP)


def decode(q, unit):
    return q.astype(F32) * unit


def kernel(
    sizes, scale, widths,
    u_ref, vel_ref, rate_ref, picks_ref, win_ref, wout_ref,
    adv_ref, gin_ref, gout_ref,
    snaps, vel, rate, hx, hx_out, hu, hu_out, hy_out, hy, hz_out, hz, hot_t, xin, wts, pre, hid, pf, tgt,
    p_out, p_in, p_unit_out, p_unit_in, res, g, core_in, q_out, q_in, u_out, u_in,
    halo_s, halo_r, x_s, x_r, w_s, w_r, p_s, p_r, r_s, r_r, g_s, g_r, loc,
):
    T, NY, NZ = sizes
    gx, gy, gz = lax.axis_index("gx"), lax.axis_index("gy"), lax.axis_index("gz")
    CX, CY, PEN = vel.shape[1:]
    rows = CX * CY
    S = hot_t.shape[0]
    Hc, IN = win_ref.shape
    NI = IN // PEN
    NE = NY * 2
    gxh, gxl = gx // 2, gx % 2
    me_e = gy * 2 + gxl
    wbits = [("gz", b) for b in range(log2(NZ))] + [("gx", b) for b in range(1, log2(T))]
    nw = len(wbits)
    NW = 1 << nw
    index = {"gx": gx, "gy": gy, "gz": gz}
    mb = [(index[a] // (1 << b)) % 2 for a, b in wbits]
    me_w = sum(mb[i] * (1 << (nw - 1 - i)) for i in range(nw))

    def w_partner(i):
        a, b = wbits[i]
        return {a: index[a] + (1 - 2 * mb[i]) * (1 << b)}

    e_pairs, straight = [], []
    for dy in range(NY):
        for dx in range(2):
            if dy or dx:
                lo = (gxl + dx) % 2
                to = {"gy": (gy + dy) % NY, "gx": gxh * 2 + lo}
                e_pairs.append((to, ((gy + dy) % NY) * 2 + lo, ((gy + NY - dy) % NY) * 2 + lo))
                straight.append(dy == 0 or dx == 0)
    e_pairs, straight = e_pairs[::-1], straight[::-1]
    NP = NE - 1
    NEAR = NP - 1

    sides = [
        ({"gx": (gx + 1) % T}, {"gx": (gx + T - 1) % T}),
        ({"gy": (gy + 1) % NY}, {"gy": (gy + NY - 1) % NY}),
        ({"gz": (gz + 1) % NZ}, {"gz": (gz + NZ - 1) % NZ}),
    ]

    def remote(src, dst, ss, rs, dev):
        return pltpu.make_async_remote_copy(
            src_ref=src, dst_ref=dst, send_sem=ss, recv_sem=rs,
            device_id=dev, device_id_type=pl.DeviceIdType.MESH,
        )

    load_u = pltpu.make_async_copy(u_ref, snaps.at[0], loc.at[0])
    load_v = pltpu.make_async_copy(vel_ref, vel, loc.at[1])
    load_r = pltpu.make_async_copy(rate_ref, rate, loc.at[2])
    NM = NI + 1
    sources = [win_ref.at[:, pl.ds(i * PEN, PEN)] for i in range(NI)] + [wout_ref]
    load_w = [pltpu.make_async_copy(sources[i], wts.at[i, me_w], loc.at[3 + i]) for i in range(NM)]
    load_u.start()
    load_v.start()
    load_r.start()
    for c in load_w:
        c.start()

    barrier = pltpu.get_barrier_semaphore()
    greet = [p[0] for p in e_pairs] + [w_partner(i) for i in range(nw)]
    for pair in sides:
        greet += list(pair)
    for dev in greet:
        pl.semaphore_signal(barrier, inc=1, device_id=dev, device_id_type=pl.DeviceIdType.MESH)
    pl.semaphore_wait(barrier, len(greet))

    WP = PEN // PARTS
    pieces = [(m, part) for m in range(NM) for part in range(PARTS)]

    def w_copy(n, stage):
        m, part = pieces[n]
        cols = pl.ds(part * WP, WP)
        i = nw - 1 - stage
        size = 1 << stage
        base = sum(mb[j] * (1 << (nw - 1 - j)) for j in range(i + 1))
        theirs = base + (1 - 2 * mb[i]) * size
        sems = (w_s.at[n, stage], w_r.at[n, stage])
        if stage == 0:
            src = win_ref.at[:, pl.ds(m * PEN + part * WP, WP)] if m < NI else wout_ref.at[:, cols]
            send = remote(src, wts.at[m, me_w, :, cols], *sems, w_partner(i))
        else:
            mine = wts.at[m, pl.ds(base, size), :, cols]
            send = remote(mine, mine, *sems, w_partner(i))
        other = wts.at[m, pl.ds(theirs, size), :, cols]
        recv = remote(other, other, *sems, w_partner(i))
        return send, recv

    def w_start(n, stage):
        if stage == 1 and n % PARTS == 0:
            load_w[n // PARTS].wait()
        w_copy(n, stage)[0].start()

    def w_next(n, stage):
        w_copy(n, stage - 1)[1].wait_recv()
        if stage < nw:
            w_start(n, stage)

    def w_inner(group):
        for n in group:
            for stage in range(2, nw):
                w_next(n, stage)

    def w_last(group):
        if nw > 1:
            for n in group:
                w_next(n, nw)

    NQ = len(pieces)
    of_in0 = range(PARTS)
    of_in1 = range(PARTS, NI * PARTS)
    of_out = range(NI * PARTS, NQ)

    def halo(step):
        faces = [
            (hx_out.at[step, 0], hx.at[step, 0], sides[0][0]),
            (hx_out.at[step, 1], hx.at[step, 1], sides[0][1]),
            (hu_out.at[step, 0], hu.at[step, 0], sides[0][0]),
            (hu_out.at[step, 1], hu.at[step, 1], sides[0][1]),
            (hy_out.at[step, 0], hy.at[step, 0], sides[1][0]),
            (hy_out.at[step, 1], hy.at[step, 1], sides[1][1]),
            (hz_out.at[step, 0], hz.at[step, 0], sides[2][0]),
            (hz_out.at[step, 1], hz.at[step, 1], sides[2][1]),
        ]
        return [
            remote(s, d, halo_s.at[step, i], halo_r.at[step, i], dev)
            for i, (s, d, dev) in enumerate(faces)
        ]

    lane = lax.broadcasted_iota(jnp.int32, (CY, 128), 1)

    def halo_x(step):
        copies = halo(step)
        for side, i in enumerate((CX - 1, 0)):
            q, unit = encode(snaps[step, pl.ds(i * CY, CY), :])
            hx_out[step, side] = q
            hu_out[step, side] = unit
            copies[side].start()
            copies[2 + side].start()

    def halo_yz(step):
        copies = halo(step)
        lo = jnp.zeros((CY, 128), F32)
        hi = jnp.zeros((CY, 128), F32)
        for i in range(CX):
            hy_out[step, 0, pl.ds(i, 1), :] = snaps[step, pl.ds(i * CY + CY - 1, 1), :]
            hy_out[step, 1, pl.ds(i, 1), :] = snaps[step, pl.ds(i * CY, 1), :]
            last = snaps[step, pl.ds(i * CY, CY), pl.ds(PEN - 128, 128)]
            head = snaps[step, pl.ds(i * CY, CY), pl.ds(0, 128)]
            hi = jnp.where(lane == i, pltpu.roll(last, i + 1, 1), hi)
            lo = jnp.where(lane == i, pltpu.roll(head, i, 1) if i else head, lo)
        hz_out[step, 0] = hi
        hz_out[step, 1] = lo
        for c in copies[4:]:
            c.start()

    row_id = lax.broadcasted_iota(jnp.int32, (CY, PEN), 0)
    lane_id = lax.broadcasted_iota(jnp.int32, (CY, PEN), 1)

    def layer(step, i):
        if i < 0:
            return decode(hx[step, 0], hu[step, 0])
        if i >= CX:
            return decode(hx[step, 1], hu[step, 1])
        return snaps[step, pl.ds(i * CY, CY), :]

    def advance(step, i):
        u = layer(step, i)
        xp, xm = layer(step, i + 1), layer(step, i - 1)
        yp = jnp.where(row_id == CY - 1, hy[step, 1, pl.ds(i, 1), :], pltpu.roll(u, CY - 1, 0))
        ym = jnp.where(row_id == 0, hy[step, 0, pl.ds(i, 1), :], pltpu.roll(u, 1, 0))
        zhi = hz[step, 1][:, i:i + 1]
        zlo = hz[step, 0][:, i:i + 1]
        zp = jnp.where(lane_id == PEN - 1, zhi, pltpu.roll(u, PEN - 1, 1))
        zm = jnp.where(lane_id == 0, zlo, pltpu.roll(u, 1, 1))
        lap = (xp + xm) + (yp + ym) + (zp + zm) - 6.0 * u
        adv = vel[0, i] * (xp - xm) + vel[1, i] * (yp - ym) + vel[2, i] * (zp - zm)
        new = u + TIME_STEP * (lap - 0.5 * adv - rate[i] * u)
        snaps[step + 1, pl.ds(i * CY, CY), :] = new

    def inner(step):
        for c in halo(step)[4:]:
            c.wait_recv()
        for i in range(1, CX - 1):
            advance(step, i)

    def outer(step):
        for c in halo(step)[:4]:
            c.wait_recv()
        for i in sorted({0, CX - 1}):
            advance(step, i)

    def x_copy(n, k):
        to, _, src = e_pairs[k]
        cols = pl.ds(n * PEN, PEN)
        sems = (x_s.at[n, k], x_r.at[n, k])
        own = me_e
        if n < RELAYED and not straight[k]:
            to, own = {"gy": to["gy"]}, gy * 2 + (1 - gxl)
        mine, other = xin.at[own, :, cols], xin.at[src, :, cols]
        return remote(mine, mine, *sems, to), remote(other, other, *sems, to)

    def pick(n):
        xin[me_e, :, pl.ds(n * PEN, PEN)] = mm(hot_t[...], snaps[n + 1].astype(BF16)).astype(BF16)

    def send_picked(n):
        for k in range(NP):
            if n >= RELAYED or straight[k]:
                x_copy(n, k)[0].start()

    def x_forward(n):
        if n < RELAYED:
            x_copy(n, NEAR)[1].wait_recv()
            for k in range(NP):
                if not straight[k]:
                    x_copy(n, k)[0].start()

    def x_wait(n):
        for k in range(NP):
            if n >= RELAYED or k != NEAR:
                x_copy(n, k)[1].wait_recv()

    load_u.wait()
    halo_x(0)
    for n in range(FIRST):
        w_start(n, 0)
    halo_yz(0)
    hot = jnp.where(
        lax.broadcasted_iota(jnp.int32, (rows, S), 0) == picks_ref[...], 1.0, 0.0
    )
    hot_t[...] = jnp.transpose(hot).astype(BF16)
    load_v.wait()
    load_r.wait()
    inner(0)
    outer(0)
    halo_x(1)
    halo_yz(1)
    pick(0)
    if EARLY:
        send_picked(0)
    for n in of_in0:
        w_next(n, 1)
    for n in range(FIRST, SECOND):
        w_start(n, 0)
    inner(1)
    outer(1)
    if not EARLY:
        send_picked(0)
    pick(1)
    send_picked(1)
    x_forward(0)
    for n in range(SECOND, NQ):
        w_start(n, 0)
    for n in of_in1:
        w_next(n, 1)
    w_inner(of_in0)
    for n in of_out:
        w_next(n, 1)
    halo_x(2)
    halo_yz(2)
    w_inner(of_in1)
    x_forward(1)
    w_last(of_in0)

    SA = NE * S
    PH = PEN // PARTS
    cb = 4 if NW % 4 == 0 else NW
    HB = cb * Hc
    NB = NW // cb

    def weight(m, b):
        return wts[m, pl.ds(b * cb, cb)].reshape(HB, PEN)

    def x_half(n):
        return xin[:, :, pl.ds(n * PEN, PEN)].reshape(SA, PEN)

    x_wait(0)
    for b in range(NB):
        pre[pl.ds(b * cb, cb)] = mm(weight(0, b), x_half(0), NT).reshape(cb, Hc, SA)
    w_inner(of_out)
    w_last(of_in1)

    def part_cols(h):
        return pl.ds(h * PH, PH)

    def p_copies(h, k):
        to = e_pairs[k][0]
        return (
            remote(p_out.at[h, k], p_in.at[h, k], p_s.at[0, h, k], p_r.at[0, h, k], to),
            remote(p_unit_out.at[h, k], p_unit_in.at[h, k], p_s.at[1, h, k], p_r.at[1, h, k], to),
        )

    x_wait(1)
    for b in range(NB):
        blk = pl.ds(b * cb, cb)
        v = pre[blk].reshape(HB, SA) + mm(weight(1, b), x_half(1), NT)
        pre[blk] = v.reshape(cb, Hc, SA)
        hid[blk] = (v / (1.0 + jnp.exp(-v))).astype(BF16).reshape(cb, Hc, SA)
    for h in range(PARTS):
        w_last(of_out[h:h + 1])
        pf[:, :, part_cols(h)] = mm(
            hid[...].reshape(NW * Hc, SA), wts[NI, :, :, part_cols(h)].reshape(NW * Hc, PH), TN
        ).reshape(NE, S, PH)
        for k in range(NP):
            q, unit = encode(pf[e_pairs[k][1], :, part_cols(h)])
            p_out[h, k] = q
            p_unit_out[h, k] = unit
            for c in p_copies(h, k):
                c.start()

    inner(2)
    outer(2)
    snap3 = snaps[STEPS]
    adv_ref[...] = snap3.reshape(CX, CY, PEN)
    hi = snap3.astype(BF16)
    rest = snap3 - hi.astype(F32)
    mid = rest.astype(BF16)
    low = (rest - mid.astype(F32)).astype(BF16)
    ht = hot_t[...]
    tgt[...] = (mm(ht, hi) + mm(ht, mid)) + mm(ht, low)

    for step in range(STEPS):
        for cp in halo(step):
            cp.wait_send()
    for n in range(NQ):
        if nw == 1 and n % PARTS == 0:
            load_w[n // PARTS].wait()
        for stage in range(nw):
            w_copy(n, stage)[0].wait_send()
    for k in range(NP):
        for n in range(NI):
            x_copy(n, k)[0].wait_send()

    def r_copy(h, k):
        to, _, src = e_pairs[k]
        sems = (r_s.at[h, k], r_r.at[h, k])
        mine, other = res.at[h, me_e], res.at[h, src]
        return remote(mine, mine, *sems, to), remote(other, other, *sems, to)

    for h in range(PARTS):
        total = pf[me_e, :, part_cols(h)] - tgt[:, part_cols(h)]
        for k in range(NP):
            for c in p_copies(h, k):
                c.wait_recv()
            total = total + decode(p_in[h, k], p_unit_in[h, k])
        res[h, me_e] = (total * scale).astype(BF16)
        for k in range(NP):
            r_copy(h, k)[0].start()

    for b in range(NB):
        blk = pl.ds(b * cb, cb)
        v = pre[blk]
        sig = 1.0 / (1.0 + jnp.exp(-v))
        pre[blk] = sig * (1.0 + v * (1.0 - sig))

    for k in range(NP):
        for h in range(PARTS):
            for cp in p_copies(h, k):
                cp.wait_send()

    starts = [sum(widths[:c]) for c in range(len(widths))]

    def cols_of(c):
        return pl.ds(starts[c], widths[c])

    def q_rows(stage):
        return sum((NW >> (s + 1)) for s in range(1, stage))

    def core_copy(c):
        half = NW // 2
        return remote(
            g.at[pl.ds((1 - mb[0]) * half, half), :, cols_of(c)], core_in.at[:, :, cols_of(c)],
            g_s.at[0, 0, c], g_r.at[0, 0, c], w_partner(0),
        )

    def bit(i):
        return 1 << (nw - 1 - i)

    orders = [
        [0] + (list(range(nw - 1, 0, -1)) if c in SWAPPED else list(range(1, nw)))
        for c in range(len(widths))
    ]

    def stage_copies(c, stage):
        size = NW >> (stage + 1)
        blk = pl.ds(q_rows(stage), size)
        one = pl.ds(stage - 1, 1)
        to = w_partner(orders[c][stage])
        return (
            remote(q_out.at[blk, :, cols_of(c)], q_in.at[blk, :, cols_of(c)],
                   g_s.at[stage, 0, c], g_r.at[stage, 0, c], to),
            remote(u_out.at[one, :, cols_of(c)], u_in.at[one, :, cols_of(c)],
                   g_s.at[stage, 1, c], g_r.at[stage, 1, c], to),
        )

    def put(c, val):
        g[:, :, cols_of(c)] = val.reshape(NW, Hc, widths[c])
        core_copy(c).start()

    def reduce(c, stage):
        cols = cols_of(c)
        order = orders[c]
        rest = order[stage + 1:]
        base = sum(mb[i] * bit(i) for i in order[:stage + 1])
        if stage == 0:
            core_copy(c).wait_recv()
        else:
            for cp in stage_copies(c, stage):
                cp.wait_recv()
            unit = u_in[stage - 1, :, cols]

        def added(vals):
            place = sum(v * bit(i) for v, i in zip(vals, rest))
            if stage == 0:
                came = core_in[place, :, cols]
            else:
                slot = q_rows(stage) + sum(v * (1 << (len(rest) - 1 - t)) for t, v in enumerate(vals))
                came = decode(q_in[slot, :, cols], unit)
            return base + place, g[base + place, :, cols] + came

        if not rest:
            val = added([])[1]
            if starts[c] < PEN:
                gout_ref[:, cols] = val
            else:
                gin_ref[:, pl.ds(starts[c] - PEN, widths[c])] = val
            return
        nxt = mb[rest[0]]
        n = len(rest) - 1
        tails = [[(k >> (n - 1 - t)) & 1 for t in range(n)] for k in range(1 << n)]
        away = [added([1 - nxt] + tail)[1] for tail in tails]
        codes, unit_out = encode_all(away)
        for k, q in enumerate(codes):
            q_out[q_rows(stage + 1) + k, :, cols] = q
        u_out[stage, :, cols] = unit_out
        for cp in stage_copies(c, stage + 1):
            cp.start()
        for tail in tails:
            place, val = added([nxt] + tail)
            g[place, :, cols] = val

    C = len(widths)
    first = [c for c in range(C) if starts[c] < PEN]
    reduced = 0
    for h in range(PARTS):
        for k in range(NP):
            r_copy(h, k)[1].wait_recv()
        for c in first:
            if starts[c] // PH == h:
                r = res[h, :, :, pl.ds(starts[c] - h * PH, widths[c])].reshape(SA, widths[c])
                put(c, mm(hid[...].reshape(NW * Hc, SA), r))
        if h < PARTS - 1:
            while reduced < len(first) and starts[reduced] // PH == h:
                reduce(reduced, 0)
                reduced += 1
    for b in range(NB):
        blk = pl.ds(b * cb, cb)
        back = sum(
            mm(wts[NI, blk, :, part_cols(h)].reshape(HB, PH), res[h].reshape(SA, PH), NT)
            for h in range(PARTS)
        )
        hid[blk] = (back * pre[blk].reshape(HB, SA)).astype(BF16).reshape(cb, Hc, SA)
        while b == 0 and reduced < len(first):
            reduce(reduced, 0)
            reduced += 1
    seconds = 0
    for c in range(len(first), C):
        x = xin[:, :, pl.ds(starts[c] - PEN, widths[c])].reshape(SA, widths[c])
        put(c, mm(hid[...].reshape(NW * Hc, SA), x))
        if reduced < c:
            reduce(reduced, 0)
            reduced += 1
        if nw > 1 and AHEAD <= c - len(first) and seconds < len(first) - 1:
            reduce(seconds, 1)
            seconds += 1
    while reduced < C:
        reduce(reduced, 0)
        reduced += 1
    for k in range(NP):
        for h in range(PARTS):
            r_copy(h, k)[0].wait_send()

    def sent(c):
        core_copy(c).wait_send()
        for stage in range(1, nw):
            for cp in stage_copies(c, stage):
                cp.wait_send()

    for t in range(C + LAG * nw):
        for stage in range(1, nw):
            c = t - LAG * (stage - 1)
            if 0 <= c < C and (stage > 1 or c >= seconds):
                reduce(c, stage)
        if 0 <= t - LAG * (nw - 1) < C - LAG:
            sent(t - LAG * (nw - 1))

    for c in range(C):
        if c >= C - LAG:
            sent(c)


def finish(*refs):
    n = (len(refs) - 1) // 2
    sems = refs[-1]
    copies = [pltpu.make_async_copy(refs[i], refs[n + i], sems.at[i]) for i in range(n)]
    for c in copies:
        c.start()
    for c in copies:
        c.wait()


def shards(sizes, scalar_field, velocity, reaction_rate, sample_cells, weight_in, weight_out):
    T, NY, NZ = sizes
    NE = NY * 2
    NW = NZ * (T // 2)
    NP = NE - 1
    nw = log2(NW)
    CX, CY, PEN = scalar_field.shape
    S = sample_cells.shape[-1]
    SA = NE * S
    PH = PEN // PARTS
    Hc, IN = weight_in.shape
    NI = IN // PEN
    NM = NI + 1
    wide = IN + PEN
    W = PEN // 2
    widths = (W,) * (wide // W)
    C = len(widths)
    scale = 1.0 / math.sqrt(S * T * NY * NZ)
    rows = CX * CY
    dma = pltpu.SemaphoreType.DMA
    vmem = pl.BlockSpec(memory_space=pltpu.VMEM)
    hbm = pl.BlockSpec(memory_space=pltpu.HBM)
    shapes = ((CX, CY, PEN), (Hc, IN), (Hc, PEN))
    outs = (pl.pallas_call(
        functools.partial(kernel, sizes, scale, widths),
        out_shape=tuple(pltpu.VMEM(s, F32) for s in shapes),
        in_specs=[hbm, hbm, hbm, vmem, hbm, hbm],
        out_specs=(vmem,) * 3,
        scratch_shapes=[
            pltpu.VMEM((STEPS + 1, rows, PEN), F32),
            pltpu.VMEM((3, CX, CY, PEN), F32),
            pltpu.VMEM((CX, CY, PEN), F32),
            pltpu.VMEM((STEPS, 2, CY, PEN), I16),
            pltpu.VMEM((STEPS, 2, CY, PEN), I16),
            pltpu.VMEM((STEPS, 2, 1, PEN), F32),
            pltpu.VMEM((STEPS, 2, 1, PEN), F32),
            pltpu.VMEM((STEPS, 2, CX, PEN), F32),
            pltpu.VMEM((STEPS, 2, CX, PEN), F32),
            pltpu.VMEM((STEPS, 2, CY, 128), F32),
            pltpu.VMEM((STEPS, 2, CY, 128), F32),
            pltpu.VMEM((S, rows), BF16),
            pltpu.VMEM((NE, S, IN), BF16),
            pltpu.VMEM((NM, NW, Hc, PEN), BF16),
            pltpu.VMEM((NW, Hc, SA), F32),
            pltpu.VMEM((NW, Hc, SA), BF16),
            pltpu.VMEM((NE, S, PEN), F32),
            pltpu.VMEM((S, PEN), F32),
            pltpu.VMEM((PARTS, NP, S, PH), I16),
            pltpu.VMEM((PARTS, NP, S, PH), I16),
            pltpu.VMEM((PARTS, NP, 1, PH), F32),
            pltpu.VMEM((PARTS, NP, 1, PH), F32),
            pltpu.VMEM((PARTS, NE, S, PH), BF16),
            pltpu.VMEM((NW, Hc, wide), F32),
            pltpu.VMEM((NW // 2, Hc, wide), F32),
            pltpu.VMEM((NW // 2 - 1, Hc, wide), I16),
            pltpu.VMEM((NW // 2 - 1, Hc, wide), I16),
            pltpu.VMEM((nw - 1, 1, wide), F32),
            pltpu.VMEM((nw - 1, 1, wide), F32),
            dma((STEPS, 8)), dma((STEPS, 8)),
            dma((NI, NP)), dma((NI, NP)),
            dma((NM * PARTS, nw)), dma((NM * PARTS, nw)),
            dma((2, PARTS, NP)), dma((2, PARTS, NP)),
            dma((PARTS, NP)), dma((PARTS, NP)),
            dma((nw, 2, C)), dma((nw, 2, C)),
            dma((3 + NM,)),
        ],
        compiler_params=pltpu.CompilerParams(
            collective_id=0, has_side_effects=True, vmem_limit_bytes=56 * 1024 * 1024
        ),
    )(
        scalar_field.reshape(rows, PEN), velocity, reaction_rate,
        sample_cells.reshape(1, S), weight_in, weight_out,
    ))
    outs = tuple(pltpu.with_memory_space_constraint(o, pltpu.VMEM) for o in outs)
    return tuple(pl.pallas_call(
        finish,
        out_shape=tuple(jax.ShapeDtypeStruct(s, F32) for s in shapes),
        in_specs=[vmem] * 3,
        out_specs=(hbm,) * 3,
        scratch_shapes=[dma((3,))],
    )(*outs))


def solution(mesh):
    sizes = (mesh.shape["gx"], mesh.shape["gy"], mesh.shape["gz"])
    in_specs = (
        P("gx", "gy", "gz"),
        P(None, "gx", "gy", "gz"),
        P("gx", "gy", "gz"),
        P("gx", "gy", "gz"),
        P(("gx", "gy", "gz"), None),
        P(("gx", "gy", "gz"), None),
    )
    out_specs = (P("gx", "gy", "gz"), P(("gx", "gy", "gz"), None), P(("gx", "gy", "gz"), None))
    return jax.shard_map(
        functools.partial(shards, sizes), mesh=mesh, in_specs=in_specs, out_specs=out_specs,
        check_vma=False,
    )
```

```python
import functools
import math

import jax
import jax.numpy as jnp
from jax import lax
from jax.experimental import pallas as pl
from jax.experimental.pallas import tpu as pltpu
from jax.sharding import PartitionSpec as P

STEPS = 3
FIRST, SECOND, EARLY = 3, 6, True
TIME_STEP = 0.15
PARTS = 2
LAG = 2
AHEAD = 2
SWAPPED = ()
RELAYED = 1
NT = (((1,), (1,)), ((), ()))
TN = (((0,), (0,)), ((), ()))
F32 = jnp.float32
BF16 = jnp.bfloat16
I16 = jnp.int16
TOP = 32766.0
TINY = 1e-30


def mm(a, b, dims=None):
    if dims is None:
        return jnp.dot(a, b, preferred_element_type=F32)
    return lax.dot_general(a, b, dims, preferred_element_type=F32)


def log2(n):
    bits = n.bit_length() - 1
    assert 1 << bits == n
    return bits


def encode(x):
    top = jnp.maximum(jnp.max(jnp.abs(x), axis=0, keepdims=True), TINY)
    return jnp.round(x * (TOP / top)).astype(I16), top * (1.0 / TOP)


def encode_all(parts):
    top = TINY
    for x in parts:
        top = jnp.maximum(top, jnp.max(jnp.abs(x), axis=0, keepdims=True))
    by = TOP / top
    return [jnp.round(x * by).astype(I16) for x in parts], top * (1.0 / TOP)


def decode(q, unit):
    return q.astype(F32) * unit


def kernel(
    sizes, scale, widths,
    u_ref, vel_ref, rate_ref, picks_ref, win_ref, wout_ref,
    adv_ref, gin_ref, gout_ref,
    snaps, vel, rate, hx, hx_out, hu, hu_out, hy_out, hy, hz_out, hz, hot_t, xin, wts, pre, hid, pf, tgt,
    p_out, p_in, p_unit_out, p_unit_in, res, g, core_in, q_out, q_in, u_out, u_in,
    halo_s, halo_r, x_s, x_r, w_s, w_r, p_s, p_r, r_s, r_r, g_s, g_r, loc,
):
    T, NY, NZ = sizes
    gx, gy, gz = lax.axis_index("gx"), lax.axis_index("gy"), lax.axis_index("gz")
    CX, CY, PEN = vel.shape[1:]
    rows = CX * CY
    S = hot_t.shape[0]
    Hc, IN = win_ref.shape
    NI = IN // PEN
    NE = NY * 2
    gxh, gxl = gx // 2, gx % 2
    me_e = gy * 2 + gxl
    wbits = [("gz", b) for b in range(log2(NZ))] + [("gx", b) for b in range(1, log2(T))]
    nw = len(wbits)
    NW = 1 << nw
    index = {"gx": gx, "gy": gy, "gz": gz}
    mb = [(index[a] // (1 << b)) % 2 for a, b in wbits]
    me_w = sum(mb[i] * (1 << (nw - 1 - i)) for i in range(nw))

    def w_partner(i):
        a, b = wbits[i]
        return {a: index[a] + (1 - 2 * mb[i]) * (1 << b)}

    e_pairs, straight = [], []
    for dy in range(NY):
        for dx in range(2):
            if dy or dx:
                lo = (gxl + dx) % 2
                to = {"gy": (gy + dy) % NY, "gx": gxh * 2 + lo}
                e_pairs.append((to, ((gy + dy) % NY) * 2 + lo, ((gy + NY - dy) % NY) * 2 + lo))
                straight.append(dy == 0 or dx == 0)
    e_pairs, straight = e_pairs[::-1], straight[::-1]
    NP = NE - 1
    NEAR = NP - 1

    sides = [
        ({"gx": (gx + 1) % T}, {"gx": (gx + T - 1) % T}),
        ({"gy": (gy + 1) % NY}, {"gy": (gy + NY - 1) % NY}),
        ({"gz": (gz + 1) % NZ}, {"gz": (gz + NZ - 1) % NZ}),
    ]

    def remote(src, dst, ss, rs, dev):
        return pltpu.make_async_remote_copy(
            src_ref=src, dst_ref=dst, send_sem=ss, recv_sem=rs,
            device_id=dev, device_id_type=pl.DeviceIdType.MESH,
        )

    load_u = pltpu.make_async_copy(u_ref, snaps.at[0], loc.at[0])
    load_v = pltpu.make_async_copy(vel_ref, vel, loc.at[1])
    load_r = pltpu.make_async_copy(rate_ref, rate, loc.at[2])
    NM = NI + 1
    WP = PEN // PARTS
    load_w = []
    for m in range(NM):
        for part in range(PARTS):
            src = win_ref.at[:, pl.ds(m * PEN + part * WP, WP)] if m < NI else wout_ref.at[:, pl.ds(part * WP, WP)]
            load_w.append(pltpu.make_async_copy(src, wts.at[m, part, me_w], loc.at[3 + m * PARTS + part]))
    load_u.start()
    load_v.start()
    load_r.start()
    for c in load_w:
        c.start()

    barrier = pltpu.get_barrier_semaphore()
    greet = [p[0] for p in e_pairs] + [w_partner(i) for i in range(nw)]
    for pair in sides:
        greet += list(pair)
    for dev in greet:
        pl.semaphore_signal(barrier, inc=1, device_id=dev, device_id_type=pl.DeviceIdType.MESH)
    pl.semaphore_wait(barrier, len(greet))

    pieces = [(m, part) for m in range(NM) for part in range(PARTS)]

    def w_copy(n, stage):
        m, part = pieces[n]
        i = nw - 1 - stage
        size = 1 << stage
        base = sum(mb[j] * (1 << (nw - 1 - j)) for j in range(i + 1))
        theirs = base + (1 - 2 * mb[i]) * size
        sems = (w_s.at[n, stage], w_r.at[n, stage])
        mine, other = wts.at[m, part, pl.ds(base, size)], wts.at[m, part, pl.ds(theirs, size)]
        return remote(mine, mine, *sems, w_partner(i)), remote(other, other, *sems, w_partner(i))

    def w_start(n, stage):
        if stage == 0:
            load_w[n].wait()
        w_copy(n, stage)[0].start()

    def w_next(n, stage):
        w_copy(n, stage - 1)[1].wait_recv()
        if stage < nw:
            w_start(n, stage)

    def w_inner(group):
        for n in group:
            for stage in range(2, nw):
                w_next(n, stage)

    def w_last(group):
        if nw > 1:
            for n in group:
                w_next(n, nw)

    NQ = len(pieces)
    of_in0 = range(PARTS)
    of_in1 = range(PARTS, NI * PARTS)
    of_out = range(NI * PARTS, NQ)

    def halo(step):
        faces = [
            (hx_out.at[step, 0], hx.at[step, 0], sides[0][0]),
            (hx_out.at[step, 1], hx.at[step, 1], sides[0][1]),
            (hu_out.at[step, 0], hu.at[step, 0], sides[0][0]),
            (hu_out.at[step, 1], hu.at[step, 1], sides[0][1]),
            (hy_out.at[step, 0], hy.at[step, 0], sides[1][0]),
            (hy_out.at[step, 1], hy.at[step, 1], sides[1][1]),
            (hz_out.at[step, 0], hz.at[step, 0], sides[2][0]),
            (hz_out.at[step, 1], hz.at[step, 1], sides[2][1]),
        ]
        return [
            remote(s, d, halo_s.at[step, i], halo_r.at[step, i], dev)
            for i, (s, d, dev) in enumerate(faces)
        ]

    lane = lax.broadcasted_iota(jnp.int32, (CY, 128), 1)

    def halo_x(step):
        copies = halo(step)
        for side, i in enumerate((CX - 1, 0)):
            q, unit = encode(snaps[step, pl.ds(i * CY, CY), :])
            hx_out[step, side] = q
            hu_out[step, side] = unit
            copies[side].start()
            copies[2 + side].start()

    def halo_yz(step):
        copies = halo(step)
        lo = jnp.zeros((CY, 128), F32)
        hi = jnp.zeros((CY, 128), F32)
        for i in range(CX):
            hy_out[step, 0, pl.ds(i, 1), :] = snaps[step, pl.ds(i * CY + CY - 1, 1), :]
            hy_out[step, 1, pl.ds(i, 1), :] = snaps[step, pl.ds(i * CY, 1), :]
            last = snaps[step, pl.ds(i * CY, CY), pl.ds(PEN - 128, 128)]
            head = snaps[step, pl.ds(i * CY, CY), pl.ds(0, 128)]
            hi = jnp.where(lane == i, pltpu.roll(last, i + 1, 1), hi)
            lo = jnp.where(lane == i, pltpu.roll(head, i, 1) if i else head, lo)
        hz_out[step, 0] = hi
        hz_out[step, 1] = lo
        for c in copies[4:]:
            c.start()

    row_id = lax.broadcasted_iota(jnp.int32, (CY, PEN), 0)
    lane_id = lax.broadcasted_iota(jnp.int32, (CY, PEN), 1)

    def layer(step, i):
        if i < 0:
            return decode(hx[step, 0], hu[step, 0])
        if i >= CX:
            return decode(hx[step, 1], hu[step, 1])
        return snaps[step, pl.ds(i * CY, CY), :]

    def advance(step, i):
        u = layer(step, i)
        xp, xm = layer(step, i + 1), layer(step, i - 1)
        yp = jnp.where(row_id == CY - 1, hy[step, 1, pl.ds(i, 1), :], pltpu.roll(u, CY - 1, 0))
        ym = jnp.where(row_id == 0, hy[step, 0, pl.ds(i, 1), :], pltpu.roll(u, 1, 0))
        zhi = hz[step, 1][:, i:i + 1]
        zlo = hz[step, 0][:, i:i + 1]
        zp = jnp.where(lane_id == PEN - 1, zhi, pltpu.roll(u, PEN - 1, 1))
        zm = jnp.where(lane_id == 0, zlo, pltpu.roll(u, 1, 1))
        lap = (xp + xm) + (yp + ym) + (zp + zm) - 6.0 * u
        adv = vel[0, i] * (xp - xm) + vel[1, i] * (yp - ym) + vel[2, i] * (zp - zm)
        new = u + TIME_STEP * (lap - 0.5 * adv - rate[i] * u)
        snaps[step + 1, pl.ds(i * CY, CY), :] = new

    def inner(step):
        for c in halo(step)[4:]:
            c.wait_recv()
        for i in range(1, CX - 1):
            advance(step, i)

    def outer(step):
        for c in halo(step)[:4]:
            c.wait_recv()
        for i in sorted({0, CX - 1}):
            advance(step, i)

    def x_copy(n, k):
        to, _, src = e_pairs[k]
        sems = (x_s.at[n, k], x_r.at[n, k])
        own = me_e
        if n < RELAYED and not straight[k]:
            to, own = {"gy": to["gy"]}, gy * 2 + (1 - gxl)
        mine, other = xin.at[n, own], xin.at[n, src]
        return remote(mine, mine, *sems, to), remote(other, other, *sems, to)

    def pick(n):
        xin[n, me_e] = mm(hot_t[...], snaps[n + 1].astype(BF16)).astype(BF16)

    def send_picked(n):
        for k in range(NP):
            if n >= RELAYED or straight[k]:
                x_copy(n, k)[0].start()

    def x_forward(n):
        if n < RELAYED:
            x_copy(n, NEAR)[1].wait_recv()
            for k in range(NP):
                if not straight[k]:
                    x_copy(n, k)[0].start()

    def x_wait(n):
        for k in range(NP):
            if n >= RELAYED or k != NEAR:
                x_copy(n, k)[1].wait_recv()

    load_u.wait()
    halo_x(0)
    for n in range(FIRST):
        w_start(n, 0)
    halo_yz(0)
    hot = jnp.where(
        lax.broadcasted_iota(jnp.int32, (rows, S), 0) == picks_ref[...], 1.0, 0.0
    )
    hot_t[...] = jnp.transpose(hot).astype(BF16)
    load_v.wait()
    load_r.wait()
    inner(0)
    outer(0)
    halo_x(1)
    halo_yz(1)
    pick(0)
    if EARLY:
        send_picked(0)
    for n in of_in0:
        w_next(n, 1)
    for n in range(FIRST, SECOND):
        w_start(n, 0)
    inner(1)
    outer(1)
    if not EARLY:
        send_picked(0)
    pick(1)
    send_picked(1)
    x_forward(0)
    for n in range(SECOND, NQ):
        w_start(n, 0)
    for n in of_in1:
        w_next(n, 1)
    w_inner(of_in0)
    for n in of_out:
        w_next(n, 1)
    halo_x(2)
    halo_yz(2)
    w_inner(of_in1)
    x_forward(1)
    w_last(of_in0)

    SA = NE * S
    PH = PEN // PARTS
    cb = 4 if NW % 4 == 0 else NW
    HB = cb * Hc
    NB = NW // cb

    def weight(m, b):
        blk = pl.ds(b * cb, cb)
        return jnp.concatenate([wts[m, part, blk].reshape(HB, WP) for part in range(PARTS)], axis=1)

    def x_half(n):
        return xin[n].reshape(SA, PEN)

    x_wait(0)
    for b in range(NB):
        pre[pl.ds(b * cb, cb)] = mm(weight(0, b), x_half(0), NT).reshape(cb, Hc, SA)
    w_inner(of_out)
    w_last(of_in1)

    def part_cols(h):
        return pl.ds(h * PH, PH)

    def p_copies(h, k):
        to = e_pairs[k][0]
        return (
            remote(p_out.at[h, k], p_in.at[h, k], p_s.at[0, h, k], p_r.at[0, h, k], to),
            remote(p_unit_out.at[h, k], p_unit_in.at[h, k], p_s.at[1, h, k], p_r.at[1, h, k], to),
        )

    x_wait(1)
    for b in range(NB):
        blk = pl.ds(b * cb, cb)
        v = pre[blk].reshape(HB, SA) + mm(weight(1, b), x_half(1), NT)
        pre[blk] = v.reshape(cb, Hc, SA)
        hid[blk] = (v / (1.0 + jnp.exp(-v))).astype(BF16).reshape(cb, Hc, SA)
    for h in range(PARTS):
        w_last(of_out[h:h + 1])
        pf[:, :, part_cols(h)] = mm(
            hid[...].reshape(NW * Hc, SA), wts[NI, h].reshape(NW * Hc, PH), TN
        ).reshape(NE, S, PH)
        for k in range(NP):
            q, unit = encode(pf[e_pairs[k][1], :, part_cols(h)])
            p_out[h, k] = q
            p_unit_out[h, k] = unit
            for c in p_copies(h, k):
                c.start()

    inner(2)
    outer(2)
    snap3 = snaps[STEPS]
    adv_ref[...] = snap3.reshape(CX, CY, PEN)
    hi = snap3.astype(BF16)
    rest = snap3 - hi.astype(F32)
    mid = rest.astype(BF16)
    low = (rest - mid.astype(F32)).astype(BF16)
    ht = hot_t[...]
    tgt[...] = (mm(ht, hi) + mm(ht, mid)) + mm(ht, low)

    for step in range(STEPS):
        for cp in halo(step):
            cp.wait_send()
    for n in range(NQ):
        for stage in range(nw):
            w_copy(n, stage)[0].wait_send()
    for k in range(NP):
        for n in range(NI):
            x_copy(n, k)[0].wait_send()

    def r_copy(h, k):
        to, _, src = e_pairs[k]
        sems = (r_s.at[h, k], r_r.at[h, k])
        mine, other = res.at[h, me_e], res.at[h, src]
        return remote(mine, mine, *sems, to), remote(other, other, *sems, to)

    for h in range(PARTS):
        total = pf[me_e, :, part_cols(h)] - tgt[:, part_cols(h)]
        for k in range(NP):
            for c in p_copies(h, k):
                c.wait_recv()
            total = total + decode(p_in[h, k], p_unit_in[h, k])
        res[h, me_e] = (total * scale).astype(BF16)
        for k in range(NP):
            r_copy(h, k)[0].start()

    for b in range(NB):
        blk = pl.ds(b * cb, cb)
        v = pre[blk]
        sig = 1.0 / (1.0 + jnp.exp(-v))
        pre[blk] = sig * (1.0 + v * (1.0 - sig))

    for k in range(NP):
        for h in range(PARTS):
            for cp in p_copies(h, k):
                cp.wait_send()

    starts = [sum(widths[:c]) for c in range(len(widths))]

    def cols_of(c):
        return pl.ds(starts[c], widths[c])

    def q_rows(stage):
        return sum((NW >> (s + 1)) for s in range(1, stage))

    def core_copy(c):
        half = NW // 2
        return remote(
            g.at[pl.ds((1 - mb[0]) * half, half), :, cols_of(c)], core_in.at[:, :, cols_of(c)],
            g_s.at[0, 0, c], g_r.at[0, 0, c], w_partner(0),
        )

    def bit(i):
        return 1 << (nw - 1 - i)

    orders = [
        [0] + (list(range(nw - 1, 0, -1)) if c in SWAPPED else list(range(1, nw)))
        for c in range(len(widths))
    ]

    def stage_copies(c, stage):
        size = NW >> (stage + 1)
        blk = pl.ds(q_rows(stage), size)
        one = pl.ds(stage - 1, 1)
        to = w_partner(orders[c][stage])
        return (
            remote(q_out.at[blk, :, cols_of(c)], q_in.at[blk, :, cols_of(c)],
                   g_s.at[stage, 0, c], g_r.at[stage, 0, c], to),
            remote(u_out.at[one, :, cols_of(c)], u_in.at[one, :, cols_of(c)],
                   g_s.at[stage, 1, c], g_r.at[stage, 1, c], to),
        )

    def put(c, val):
        g[:, :, cols_of(c)] = val.reshape(NW, Hc, widths[c])
        core_copy(c).start()

    def left(c, stage):
        for cp in (core_copy(c),) if stage == 0 else stage_copies(c, stage):
            cp.wait_send()

    def reduce(c, stage):
        cols = cols_of(c)
        order = orders[c]
        rest = order[stage + 1:]
        base = sum(mb[i] * bit(i) for i in order[:stage + 1])
        if stage == 0:
            core_copy(c).wait_recv()
        else:
            for cp in stage_copies(c, stage):
                cp.wait_recv()
            unit = u_in[stage - 1, :, cols]

        def added(vals):
            place = sum(v * bit(i) for v, i in zip(vals, rest))
            if stage == 0:
                came = core_in[place, :, cols]
            else:
                slot = q_rows(stage) + sum(v * (1 << (len(rest) - 1 - t)) for t, v in enumerate(vals))
                came = decode(q_in[slot, :, cols], unit)
            return base + place, g[base + place, :, cols] + came

        if not rest:
            val = added([])[1]
            if starts[c] < PEN:
                gout_ref[:, cols] = val
            else:
                gin_ref[:, pl.ds(starts[c] - PEN, widths[c])] = val
            left(c, stage)
            return
        nxt = mb[rest[0]]
        n = len(rest) - 1
        tails = [[(k >> (n - 1 - t)) & 1 for t in range(n)] for k in range(1 << n)]
        away = [added([1 - nxt] + tail)[1] for tail in tails]
        codes, unit_out = encode_all(away)
        for k, q in enumerate(codes):
            q_out[q_rows(stage + 1) + k, :, cols] = q
        u_out[stage, :, cols] = unit_out
        for cp in stage_copies(c, stage + 1):
            cp.start()
        for tail in tails:
            place, val = added([nxt] + tail)
            g[place, :, cols] = val
        left(c, stage)

    C = len(widths)
    first = [c for c in range(C) if starts[c] < PEN]
    reduced = 0
    for h in range(PARTS):
        for k in range(NP):
            r_copy(h, k)[1].wait_recv()
        for c in first:
            if starts[c] // PH == h:
                r = res[h, :, :, pl.ds(starts[c] - h * PH, widths[c])].reshape(SA, widths[c])
                put(c, mm(hid[...].reshape(NW * Hc, SA), r))
        if h < PARTS - 1:
            while reduced < len(first) and starts[reduced] // PH == h:
                reduce(reduced, 0)
                reduced += 1
    for b in range(NB):
        blk = pl.ds(b * cb, cb)
        back = sum(
            mm(wts[NI, h, blk].reshape(HB, PH), res[h].reshape(SA, PH), NT)
            for h in range(PARTS)
        )
        hid[blk] = (back * pre[blk].reshape(HB, SA)).astype(BF16).reshape(cb, Hc, SA)
        while b == 0 and reduced < len(first):
            reduce(reduced, 0)
            reduced += 1
    seconds = 0
    for c in range(len(first), C):
        at = starts[c] - PEN
        x = xin[at // PEN, :, :, pl.ds(at % PEN, widths[c])].reshape(SA, widths[c])
        put(c, mm(hid[...].reshape(NW * Hc, SA), x))
        if reduced < c:
            reduce(reduced, 0)
            reduced += 1
        if nw > 1 and AHEAD <= c - len(first) and seconds < len(first) - 1:
            reduce(seconds, 1)
            seconds += 1
    while reduced < C:
        reduce(reduced, 0)
        reduced += 1
    for k in range(NP):
        for h in range(PARTS):
            r_copy(h, k)[0].wait_send()

    for t in range(C + LAG * nw):
        for stage in range(1, nw):
            c = t - LAG * (stage - 1)
            if 0 <= c < C and (stage > 1 or c >= seconds):
                reduce(c, stage)


def finish(*refs):
    n = (len(refs) - 1) // 2
    sems = refs[-1]
    copies = [pltpu.make_async_copy(refs[i], refs[n + i], sems.at[i]) for i in range(n)]
    for c in copies:
        c.start()
    for c in copies:
        c.wait()


def shards(sizes, scalar_field, velocity, reaction_rate, sample_cells, weight_in, weight_out):
    T, NY, NZ = sizes
    NE = NY * 2
    NW = NZ * (T // 2)
    NP = NE - 1
    nw = log2(NW)
    CX, CY, PEN = scalar_field.shape
    S = sample_cells.shape[-1]
    SA = NE * S
    PH = PEN // PARTS
    Hc, IN = weight_in.shape
    NI = IN // PEN
    NM = NI + 1
    wide = IN + PEN
    W = PEN // 2
    widths = (W,) * (wide // W)
    C = len(widths)
    scale = 1.0 / math.sqrt(S * T * NY * NZ)
    rows = CX * CY
    dma = pltpu.SemaphoreType.DMA
    vmem = pl.BlockSpec(memory_space=pltpu.VMEM)
    hbm = pl.BlockSpec(memory_space=pltpu.HBM)
    shapes = ((CX, CY, PEN), (Hc, IN), (Hc, PEN))
    outs = (pl.pallas_call(
        functools.partial(kernel, sizes, scale, widths),
        out_shape=tuple(pltpu.VMEM(s, F32) for s in shapes),
        in_specs=[hbm, hbm, hbm, vmem, hbm, hbm],
        out_specs=(vmem,) * 3,
        scratch_shapes=[
            pltpu.VMEM((STEPS + 1, rows, PEN), F32),
            pltpu.VMEM((3, CX, CY, PEN), F32),
            pltpu.VMEM((CX, CY, PEN), F32),
            pltpu.VMEM((STEPS, 2, CY, PEN), I16),
            pltpu.VMEM((STEPS, 2, CY, PEN), I16),
            pltpu.VMEM((STEPS, 2, 1, PEN), F32),
            pltpu.VMEM((STEPS, 2, 1, PEN), F32),
            pltpu.VMEM((STEPS, 2, CX, PEN), F32),
            pltpu.VMEM((STEPS, 2, CX, PEN), F32),
            pltpu.VMEM((STEPS, 2, CY, 128), F32),
            pltpu.VMEM((STEPS, 2, CY, 128), F32),
            pltpu.VMEM((S, rows), BF16),
            pltpu.VMEM((NI, NE, S, PEN), BF16),
            pltpu.VMEM((NM, PARTS, NW, Hc, PEN // PARTS), BF16),
            pltpu.VMEM((NW, Hc, SA), F32),
            pltpu.VMEM((NW, Hc, SA), BF16),
            pltpu.VMEM((NE, S, PEN), F32),
            pltpu.VMEM((S, PEN), F32),
            pltpu.VMEM((PARTS, NP, S, PH), I16),
            pltpu.VMEM((PARTS, NP, S, PH), I16),
            pltpu.VMEM((PARTS, NP, 1, PH), F32),
            pltpu.VMEM((PARTS, NP, 1, PH), F32),
            pltpu.VMEM((PARTS, NE, S, PH), BF16),
            pltpu.VMEM((NW, Hc, wide), F32),
            pltpu.VMEM((NW // 2, Hc, wide), F32),
            pltpu.VMEM((NW // 2 - 1, Hc, wide), I16),
            pltpu.VMEM((NW // 2 - 1, Hc, wide), I16),
            pltpu.VMEM((nw - 1, 1, wide), F32),
            pltpu.VMEM((nw - 1, 1, wide), F32),
            dma((STEPS, 8)), dma((STEPS, 8)),
            dma((NI, NP)), dma((NI, NP)),
            dma((NM * PARTS, nw)), dma((NM * PARTS, nw)),
            dma((2, PARTS, NP)), dma((2, PARTS, NP)),
            dma((PARTS, NP)), dma((PARTS, NP)),
            dma((nw, 2, C)), dma((nw, 2, C)),
            dma((3 + NM * PARTS,)),
        ],
        compiler_params=pltpu.CompilerParams(
            collective_id=0, has_side_effects=True, vmem_limit_bytes=56 * 1024 * 1024
        ),
    )(
        scalar_field.reshape(rows, PEN), velocity, reaction_rate,
        sample_cells.reshape(1, S), weight_in, weight_out,
    ))
    outs = tuple(pltpu.with_memory_space_constraint(o, pltpu.VMEM) for o in outs)
    return tuple(pl.pallas_call(
        finish,
        out_shape=tuple(jax.ShapeDtypeStruct(s, F32) for s in shapes),
        in_specs=[vmem] * 3,
        out_specs=(hbm,) * 3,
        scratch_shapes=[dma((3,))],
    )(*outs))


def solution(mesh):
    sizes = (mesh.shape["gx"], mesh.shape["gy"], mesh.shape["gz"])
    in_specs = (
        P("gx", "gy", "gz"),
        P(None, "gx", "gy", "gz"),
        P("gx", "gy", "gz"),
        P("gx", "gy", "gz"),
        P(("gx", "gy", "gz"), None),
        P(("gx", "gy", "gz"), None),
    )
    out_specs = (P("gx", "gy", "gz"), P(("gx", "gy", "gz"), None), P(("gx", "gy", "gz"), None))
    return jax.shard_map(
        functools.partial(shards, sizes), mesh=mesh, in_specs=in_specs, out_specs=out_specs,
        check_vma=False,
    )
```

```python
import functools
import math

import jax
import jax.numpy as jnp
from jax import lax
from jax.experimental import pallas as pl
from jax.experimental.pallas import tpu as pltpu
from jax.sharding import PartitionSpec as P

STEPS = 3
FIRST, SECOND, EARLY = 3, 6, True
TIME_STEP = 0.15
PARTS = 2
LAG = 2
AHEAD = 2
SWAPPED = ()
RELAYED = 1
NT = (((1,), (1,)), ((), ()))
TN = (((0,), (0,)), ((), ()))
F32 = jnp.float32
BF16 = jnp.bfloat16
I16 = jnp.int16
TOP = 32766.0
TINY = 1e-30


def mm(a, b, dims=None):
    if dims is None:
        return jnp.dot(a, b, preferred_element_type=F32)
    return lax.dot_general(a, b, dims, preferred_element_type=F32)


def log2(n):
    bits = n.bit_length() - 1
    assert 1 << bits == n
    return bits


def encode(x):
    top = jnp.maximum(jnp.max(jnp.abs(x), axis=0, keepdims=True), TINY)
    return jnp.round(x * (TOP / top)).astype(I16), top * (1.0 / TOP)


def encode_all(parts):
    top = TINY
    for x in parts:
        top = jnp.maximum(top, jnp.max(jnp.abs(x), axis=0, keepdims=True))
    by = TOP / top
    return [jnp.round(x * by).astype(I16) for x in parts], top * (1.0 / TOP)


def decode(q, unit):
    return q.astype(F32) * unit


def kernel(
    sizes, scale, widths,
    u_ref, vel_ref, rate_ref, picks_ref, win_ref, wout_ref,
    adv_ref, gin_ref, gout_ref,
    snaps, vel, rate, hx, hx_out, hu, hu_out, hy_out, hy, hz_out, hz, hot_t, xin, wts, pre, hid, pf, tgt,
    p_out, p_in, p_unit_out, p_unit_in, res, g, core_in, q_out, q_in, u_out, u_in,
    halo_s, halo_r, x_s, x_r, w_s, w_r, p_s, p_r, r_s, r_r, g_s, g_r, loc,
):
    T, NY, NZ = sizes
    gx, gy, gz = lax.axis_index("gx"), lax.axis_index("gy"), lax.axis_index("gz")
    CX, CY, PEN = vel.shape[1:]
    rows = CX * CY
    S = hot_t.shape[0]
    Hc, IN = win_ref.shape
    NI = IN // PEN
    NE = NY * 2
    gxh, gxl = gx // 2, gx % 2
    me_e = gy * 2 + gxl
    wbits = [("gz", b) for b in range(log2(NZ))] + [("gx", b) for b in range(1, log2(T))]
    nw = len(wbits)
    NW = 1 << nw
    index = {"gx": gx, "gy": gy, "gz": gz}
    mb = [(index[a] // (1 << b)) % 2 for a, b in wbits]
    me_w = sum(mb[i] * (1 << (nw - 1 - i)) for i in range(nw))

    def w_partner(i):
        a, b = wbits[i]
        return {a: index[a] + (1 - 2 * mb[i]) * (1 << b)}

    e_pairs, straight = [], []
    for dy in range(NY):
        for dx in range(2):
            if dy or dx:
                lo = (gxl + dx) % 2
                to = {"gy": (gy + dy) % NY, "gx": gxh * 2 + lo}
                e_pairs.append((to, ((gy + dy) % NY) * 2 + lo, ((gy + NY - dy) % NY) * 2 + lo))
                straight.append(dy == 0 or dx == 0)
    e_pairs, straight = e_pairs[::-1], straight[::-1]
    NP = NE - 1
    NEAR = NP - 1

    sides = [
        ({"gx": (gx + 1) % T}, {"gx": (gx + T - 1) % T}),
        ({"gy": (gy + 1) % NY}, {"gy": (gy + NY - 1) % NY}),
        ({"gz": (gz + 1) % NZ}, {"gz": (gz + NZ - 1) % NZ}),
    ]

    def remote(src, dst, ss, rs, dev):
        return pltpu.make_async_remote_copy(
            src_ref=src, dst_ref=dst, send_sem=ss, recv_sem=rs,
            device_id=dev, device_id_type=pl.DeviceIdType.MESH,
        )

    load_u = pltpu.make_async_copy(u_ref, snaps.at[0], loc.at[0])
    load_v = pltpu.make_async_copy(vel_ref, vel, loc.at[1])
    load_r = pltpu.make_async_copy(rate_ref, rate, loc.at[2])
    NM = NI + 1
    WP = PEN // PARTS
    load_w = []
    for m in range(NM):
        for part in range(PARTS):
            src = win_ref.at[:, pl.ds(m * PEN + part * WP, WP)] if m < NI else wout_ref.at[:, pl.ds(part * WP, WP)]
            load_w.append(pltpu.make_async_copy(src, wts.at[m, part, me_w], loc.at[3 + m * PARTS + part]))
    load_u.start()
    load_v.start()
    load_r.start()
    for c in load_w:
        c.start()

    barrier = pltpu.get_barrier_semaphore()
    greet = [p[0] for p in e_pairs] + [w_partner(i) for i in range(nw)]
    for pair in sides:
        greet += list(pair)
    for dev in greet:
        pl.semaphore_signal(barrier, inc=1, device_id=dev, device_id_type=pl.DeviceIdType.MESH)
    pl.semaphore_wait(barrier, len(greet))

    pieces = [(m, part) for m in range(NM) for part in range(PARTS)]

    def w_copy(n, stage):
        m, part = pieces[n]
        i = nw - 1 - stage
        size = 1 << stage
        base = sum(mb[j] * (1 << (nw - 1 - j)) for j in range(i + 1))
        theirs = base + (1 - 2 * mb[i]) * size
        sems = (w_s.at[n, stage], w_r.at[n, stage])
        mine, other = wts.at[m, part, pl.ds(base, size)], wts.at[m, part, pl.ds(theirs, size)]
        return remote(mine, mine, *sems, w_partner(i)), remote(other, other, *sems, w_partner(i))

    def w_start(n, stage):
        if stage == 0:
            load_w[n].wait()
        w_copy(n, stage)[0].start()

    def w_next(n, stage):
        w_copy(n, stage - 1)[1].wait_recv()
        if stage < nw:
            w_start(n, stage)

    def w_inner(group):
        for n in group:
            for stage in range(2, nw):
                w_next(n, stage)

    def w_last(group):
        if nw > 1:
            for n in group:
                w_next(n, nw)

    NQ = len(pieces)
    of_in0 = range(PARTS)
    of_in1 = range(PARTS, NI * PARTS)
    of_out = range(NI * PARTS, NQ)

    def halo(step):
        faces = [
            (hx_out.at[step, 0], hx.at[step, 0], sides[0][0]),
            (hx_out.at[step, 1], hx.at[step, 1], sides[0][1]),
            (hu_out.at[step, 0], hu.at[step, 0], sides[0][0]),
            (hu_out.at[step, 1], hu.at[step, 1], sides[0][1]),
            (hy_out.at[step, 0], hy.at[step, 0], sides[1][0]),
            (hy_out.at[step, 1], hy.at[step, 1], sides[1][1]),
            (hz_out.at[step, 0], hz.at[step, 0], sides[2][0]),
            (hz_out.at[step, 1], hz.at[step, 1], sides[2][1]),
        ]
        return [
            remote(s, d, halo_s.at[step, i], halo_r.at[step, i], dev)
            for i, (s, d, dev) in enumerate(faces)
        ]

    lane = lax.broadcasted_iota(jnp.int32, (CY, 128), 1)

    def halo_x(step):
        copies = halo(step)
        for side, i in enumerate((CX - 1, 0)):
            q, unit = encode(snaps[step, pl.ds(i * CY, CY), :])
            hx_out[step, side] = q
            hu_out[step, side] = unit
            copies[side].start()
            copies[2 + side].start()

    def halo_yz(step):
        copies = halo(step)
        lo = jnp.zeros((CY, 128), F32)
        hi = jnp.zeros((CY, 128), F32)
        for i in range(CX):
            hy_out[step, 0, pl.ds(i, 1), :] = snaps[step, pl.ds(i * CY + CY - 1, 1), :]
            hy_out[step, 1, pl.ds(i, 1), :] = snaps[step, pl.ds(i * CY, 1), :]
            last = snaps[step, pl.ds(i * CY, CY), pl.ds(PEN - 128, 128)]
            head = snaps[step, pl.ds(i * CY, CY), pl.ds(0, 128)]
            hi = jnp.where(lane == i, pltpu.roll(last, i + 1, 1), hi)
            lo = jnp.where(lane == i, pltpu.roll(head, i, 1) if i else head, lo)
        hz_out[step, 0] = hi
        hz_out[step, 1] = lo
        for c in copies[4:]:
            c.start()

    row_id = lax.broadcasted_iota(jnp.int32, (CY, PEN), 0)
    lane_id = lax.broadcasted_iota(jnp.int32, (CY, PEN), 1)

    def layer(step, i):
        if i < 0:
            return decode(hx[step, 0], hu[step, 0])
        if i >= CX:
            return decode(hx[step, 1], hu[step, 1])
        return snaps[step, pl.ds(i * CY, CY), :]

    def advance(step, i):
        u = layer(step, i)
        xp, xm = layer(step, i + 1), layer(step, i - 1)
        yp = jnp.where(row_id == CY - 1, hy[step, 1, pl.ds(i, 1), :], pltpu.roll(u, CY - 1, 0))
        ym = jnp.where(row_id == 0, hy[step, 0, pl.ds(i, 1), :], pltpu.roll(u, 1, 0))
        zhi = hz[step, 1][:, i:i + 1]
        zlo = hz[step, 0][:, i:i + 1]
        zp = jnp.where(lane_id == PEN - 1, zhi, pltpu.roll(u, PEN - 1, 1))
        zm = jnp.where(lane_id == 0, zlo, pltpu.roll(u, 1, 1))
        lap = (xp + xm) + (yp + ym) + (zp + zm) - 6.0 * u
        adv = vel[0, i] * (xp - xm) + vel[1, i] * (yp - ym) + vel[2, i] * (zp - zm)
        new = u + TIME_STEP * (lap - 0.5 * adv - rate[i] * u)
        snaps[step + 1, pl.ds(i * CY, CY), :] = new

    def inner(step):
        for c in halo(step)[4:]:
            c.wait_recv()
        for i in range(1, CX - 1):
            advance(step, i)

    def outer(step):
        for c in halo(step)[:4]:
            c.wait_recv()
        for i in sorted({0, CX - 1}):
            advance(step, i)

    def x_copy(n, k):
        to, _, src = e_pairs[k]
        cols = pl.ds(n * PEN, PEN)
        sems = (x_s.at[n, k], x_r.at[n, k])
        own = me_e
        if n < RELAYED and not straight[k]:
            to, own = {"gy": to["gy"]}, gy * 2 + (1 - gxl)
        mine, other = xin.at[own, :, cols], xin.at[src, :, cols]
        return remote(mine, mine, *sems, to), remote(other, other, *sems, to)

    def pick(n):
        xin[me_e, :, pl.ds(n * PEN, PEN)] = mm(hot_t[...], snaps[n + 1].astype(BF16)).astype(BF16)

    def send_picked(n):
        for k in range(NP):
            if n >= RELAYED or straight[k]:
                x_copy(n, k)[0].start()

    def x_forward(n):
        if n < RELAYED:
            x_copy(n, NEAR)[1].wait_recv()
            for k in range(NP):
                if not straight[k]:
                    x_copy(n, k)[0].start()

    def x_wait(n):
        for k in range(NP):
            if n >= RELAYED or k != NEAR:
                x_copy(n, k)[1].wait_recv()

    load_u.wait()
    halo_x(0)
    for n in range(FIRST):
        w_start(n, 0)
    halo_yz(0)
    hot = jnp.where(
        lax.broadcasted_iota(jnp.int32, (rows, S), 0) == picks_ref[...], 1.0, 0.0
    )
    hot_t[...] = jnp.transpose(hot).astype(BF16)
    load_v.wait()
    load_r.wait()
    inner(0)
    outer(0)
    halo_x(1)
    halo_yz(1)
    pick(0)
    if EARLY:
        send_picked(0)
    for n in of_in0:
        w_next(n, 1)
    for n in range(FIRST, SECOND):
        w_start(n, 0)
    inner(1)
    outer(1)
    if not EARLY:
        send_picked(0)
    pick(1)
    send_picked(1)
    x_forward(0)
    for n in range(SECOND, NQ):
        w_start(n, 0)
    for n in of_in1:
        w_next(n, 1)
    w_inner(of_in0)
    for n in of_out:
        w_next(n, 1)
    halo_x(2)
    halo_yz(2)
    w_inner(of_in1)
    x_forward(1)
    w_last(of_in0)

    SA = NE * S
    PH = PEN // PARTS
    cb = 4 if NW % 4 == 0 else NW
    HB = cb * Hc
    NB = NW // cb

    def weight(m, b):
        blk = pl.ds(b * cb, cb)
        return jnp.concatenate([wts[m, part, blk].reshape(HB, WP) for part in range(PARTS)], axis=1)

    def x_half(n):
        return xin[:, :, pl.ds(n * PEN, PEN)].reshape(SA, PEN)

    x_wait(0)
    for b in range(NB):
        pre[pl.ds(b * cb, cb)] = mm(weight(0, b), x_half(0), NT).reshape(cb, Hc, SA)
    w_inner(of_out)
    w_last(of_in1)

    def part_cols(h):
        return pl.ds(h * PH, PH)

    def p_copies(h, k):
        to = e_pairs[k][0]
        return (
            remote(p_out.at[h, k], p_in.at[h, k], p_s.at[0, h, k], p_r.at[0, h, k], to),
            remote(p_unit_out.at[h, k], p_unit_in.at[h, k], p_s.at[1, h, k], p_r.at[1, h, k], to),
        )

    x_wait(1)
    for b in range(NB):
        blk = pl.ds(b * cb, cb)
        v = pre[blk].reshape(HB, SA) + mm(weight(1, b), x_half(1), NT)
        pre[blk] = v.reshape(cb, Hc, SA)
        hid[blk] = (v / (1.0 + jnp.exp(-v))).astype(BF16).reshape(cb, Hc, SA)
    for h in range(PARTS):
        w_last(of_out[h:h + 1])
        pf[:, :, part_cols(h)] = mm(
            hid[...].reshape(NW * Hc, SA), wts[NI, h].reshape(NW * Hc, PH), TN
        ).reshape(NE, S, PH)
        for k in range(NP):
            q, unit = encode(pf[e_pairs[k][1], :, part_cols(h)])
            p_out[h, k] = q
            p_unit_out[h, k] = unit
            for c in p_copies(h, k):
                c.start()

    inner(2)
    outer(2)
    snap3 = snaps[STEPS]
    adv_ref[...] = snap3.reshape(CX, CY, PEN)
    hi = snap3.astype(BF16)
    rest = snap3 - hi.astype(F32)
    mid = rest.astype(BF16)
    low = (rest - mid.astype(F32)).astype(BF16)
    ht = hot_t[...]
    tgt[...] = (mm(ht, hi) + mm(ht, mid)) + mm(ht, low)

    for step in range(STEPS):
        for cp in halo(step):
            cp.wait_send()
    for n in range(NQ):
        for stage in range(nw):
            w_copy(n, stage)[0].wait_send()
    for k in range(NP):
        for n in range(NI):
            x_copy(n, k)[0].wait_send()

    def r_copy(h, k):
        to, _, src = e_pairs[k]
        sems = (r_s.at[h, k], r_r.at[h, k])
        mine, other = res.at[h, me_e], res.at[h, src]
        return remote(mine, mine, *sems, to), remote(other, other, *sems, to)

    for h in range(PARTS):
        total = pf[me_e, :, part_cols(h)] - tgt[:, part_cols(h)]
        for k in range(NP):
            for c in p_copies(h, k):
                c.wait_recv()
            total = total + decode(p_in[h, k], p_unit_in[h, k])
        res[h, me_e] = (total * scale).astype(BF16)
        for k in range(NP):
            r_copy(h, k)[0].start()

    for b in range(NB):
        blk = pl.ds(b * cb, cb)
        v = pre[blk]
        sig = 1.0 / (1.0 + jnp.exp(-v))
        pre[blk] = sig * (1.0 + v * (1.0 - sig))

    for k in range(NP):
        for h in range(PARTS):
            for cp in p_copies(h, k):
                cp.wait_send()

    starts = [sum(widths[:c]) for c in range(len(widths))]

    def cols_of(c):
        return pl.ds(starts[c], widths[c])

    def q_rows(stage):
        return sum((NW >> (s + 1)) for s in range(1, stage))

    def core_copy(c):
        half = NW // 2
        return remote(
            g.at[pl.ds((1 - mb[0]) * half, half), :, cols_of(c)], core_in.at[:, :, cols_of(c)],
            g_s.at[0, 0, c], g_r.at[0, 0, c], w_partner(0),
        )

    def bit(i):
        return 1 << (nw - 1 - i)

    orders = [
        [0] + (list(range(nw - 1, 0, -1)) if c in SWAPPED else list(range(1, nw)))
        for c in range(len(widths))
    ]

    def stage_copies(c, stage):
        size = NW >> (stage + 1)
        blk = pl.ds(q_rows(stage), size)
        one = pl.ds(stage - 1, 1)
        to = w_partner(orders[c][stage])
        return (
            remote(q_out.at[blk, :, cols_of(c)], q_in.at[blk, :, cols_of(c)],
                   g_s.at[stage, 0, c], g_r.at[stage, 0, c], to),
            remote(u_out.at[one, :, cols_of(c)], u_in.at[one, :, cols_of(c)],
                   g_s.at[stage, 1, c], g_r.at[stage, 1, c], to),
        )

    def put(c, val):
        g[:, :, cols_of(c)] = val.reshape(NW, Hc, widths[c])
        core_copy(c).start()

    def reduce(c, stage):
        cols = cols_of(c)
        order = orders[c]
        rest = order[stage + 1:]
        base = sum(mb[i] * bit(i) for i in order[:stage + 1])
        if stage == 0:
            core_copy(c).wait_recv()
        else:
            for cp in stage_copies(c, stage):
                cp.wait_recv()
            unit = u_in[stage - 1, :, cols]

        def added(vals):
            place = sum(v * bit(i) for v, i in zip(vals, rest))
            if stage == 0:
                came = core_in[place, :, cols]
            else:
                slot = q_rows(stage) + sum(v * (1 << (len(rest) - 1 - t)) for t, v in enumerate(vals))
                came = decode(q_in[slot, :, cols], unit)
            return base + place, g[base + place, :, cols] + came

        if not rest:
            val = added([])[1]
            if starts[c] < PEN:
                gout_ref[:, cols] = val
            else:
                gin_ref[:, pl.ds(starts[c] - PEN, widths[c])] = val
            return
        nxt = mb[rest[0]]
        n = len(rest) - 1
        tails = [[(k >> (n - 1 - t)) & 1 for t in range(n)] for k in range(1 << n)]
        away = [added([1 - nxt] + tail)[1] for tail in tails]
        codes, unit_out = encode_all(away)
        for k, q in enumerate(codes):
            q_out[q_rows(stage + 1) + k, :, cols] = q
        u_out[stage, :, cols] = unit_out
        for cp in stage_copies(c, stage + 1):
            cp.start()
        for tail in tails:
            place, val = added([nxt] + tail)
            g[place, :, cols] = val

    C = len(widths)
    first = [c for c in range(C) if starts[c] < PEN]
    reduced = 0
    for h in range(PARTS):
        for k in range(NP):
            r_copy(h, k)[1].wait_recv()
        for c in first:
            if starts[c] // PH == h:
                r = res[h, :, :, pl.ds(starts[c] - h * PH, widths[c])].reshape(SA, widths[c])
                put(c, mm(hid[...].reshape(NW * Hc, SA), r))
        if h < PARTS - 1:
            while reduced < len(first) and starts[reduced] // PH == h:
                reduce(reduced, 0)
                reduced += 1
    for b in range(NB):
        blk = pl.ds(b * cb, cb)
        back = sum(
            mm(wts[NI, h, blk].reshape(HB, PH), res[h].reshape(SA, PH), NT)
            for h in range(PARTS)
        )
        hid[blk] = (back * pre[blk].reshape(HB, SA)).astype(BF16).reshape(cb, Hc, SA)
        while b == 0 and reduced < len(first):
            reduce(reduced, 0)
            reduced += 1
    seconds = 0
    for c in range(len(first), C):
        x = xin[:, :, pl.ds(starts[c] - PEN, widths[c])].reshape(SA, widths[c])
        put(c, mm(hid[...].reshape(NW * Hc, SA), x))
        if reduced < c:
            reduce(reduced, 0)
            reduced += 1
        if nw > 1 and AHEAD <= c - len(first) and seconds < len(first) - 1:
            reduce(seconds, 1)
            seconds += 1
    while reduced < C:
        reduce(reduced, 0)
        reduced += 1
    for k in range(NP):
        for h in range(PARTS):
            r_copy(h, k)[0].wait_send()

    def sent(c):
        core_copy(c).wait_send()
        for stage in range(1, nw):
            for cp in stage_copies(c, stage):
                cp.wait_send()

    for t in range(C + LAG * nw):
        for stage in range(1, nw):
            c = t - LAG * (stage - 1)
            if 0 <= c < C and (stage > 1 or c >= seconds):
                reduce(c, stage)
        if 0 <= t - LAG * (nw - 1) < C - LAG:
            sent(t - LAG * (nw - 1))

    for c in range(C):
        if c >= C - LAG:
            sent(c)


def finish(*refs):
    n = (len(refs) - 1) // 2
    sems = refs[-1]
    copies = [pltpu.make_async_copy(refs[i], refs[n + i], sems.at[i]) for i in range(n)]
    for c in copies:
        c.start()
    for c in copies:
        c.wait()


def shards(sizes, scalar_field, velocity, reaction_rate, sample_cells, weight_in, weight_out):
    T, NY, NZ = sizes
    NE = NY * 2
    NW = NZ * (T // 2)
    NP = NE - 1
    nw = log2(NW)
    CX, CY, PEN = scalar_field.shape
    S = sample_cells.shape[-1]
    SA = NE * S
    PH = PEN // PARTS
    Hc, IN = weight_in.shape
    NI = IN // PEN
    NM = NI + 1
    wide = IN + PEN
    W = PEN // 2
    widths = (W,) * (wide // W)
    C = len(widths)
    scale = 1.0 / math.sqrt(S * T * NY * NZ)
    rows = CX * CY
    dma = pltpu.SemaphoreType.DMA
    vmem = pl.BlockSpec(memory_space=pltpu.VMEM)
    hbm = pl.BlockSpec(memory_space=pltpu.HBM)
    shapes = ((CX, CY, PEN), (Hc, IN), (Hc, PEN))
    outs = (pl.pallas_call(
        functools.partial(kernel, sizes, scale, widths),
        out_shape=tuple(pltpu.VMEM(s, F32) for s in shapes),
        in_specs=[hbm, hbm, hbm, vmem, hbm, hbm],
        out_specs=(vmem,) * 3,
        scratch_shapes=[
            pltpu.VMEM((STEPS + 1, rows, PEN), F32),
            pltpu.VMEM((3, CX, CY, PEN), F32),
            pltpu.VMEM((CX, CY, PEN), F32),
            pltpu.VMEM((STEPS, 2, CY, PEN), I16),
            pltpu.VMEM((STEPS, 2, CY, PEN), I16),
            pltpu.VMEM((STEPS, 2, 1, PEN), F32),
            pltpu.VMEM((STEPS, 2, 1, PEN), F32),
            pltpu.VMEM((STEPS, 2, CX, PEN), F32),
            pltpu.VMEM((STEPS, 2, CX, PEN), F32),
            pltpu.VMEM((STEPS, 2, CY, 128), F32),
            pltpu.VMEM((STEPS, 2, CY, 128), F32),
            pltpu.VMEM((S, rows), BF16),
            pltpu.VMEM((NE, S, IN), BF16),
            pltpu.VMEM((NM, PARTS, NW, Hc, PEN // PARTS), BF16),
            pltpu.VMEM((NW, Hc, SA), F32),
            pltpu.VMEM((NW, Hc, SA), BF16),
            pltpu.VMEM((NE, S, PEN), F32),
            pltpu.VMEM((S, PEN), F32),
            pltpu.VMEM((PARTS, NP, S, PH), I16),
            pltpu.VMEM((PARTS, NP, S, PH), I16),
            pltpu.VMEM((PARTS, NP, 1, PH), F32),
            pltpu.VMEM((PARTS, NP, 1, PH), F32),
            pltpu.VMEM((PARTS, NE, S, PH), BF16),
            pltpu.VMEM((NW, Hc, wide), F32),
            pltpu.VMEM((NW // 2, Hc, wide), F32),
            pltpu.VMEM((NW // 2 - 1, Hc, wide), I16),
            pltpu.VMEM((NW // 2 - 1, Hc, wide), I16),
            pltpu.VMEM((nw - 1, 1, wide), F32),
            pltpu.VMEM((nw - 1, 1, wide), F32),
            dma((STEPS, 8)), dma((STEPS, 8)),
            dma((NI, NP)), dma((NI, NP)),
            dma((NM * PARTS, nw)), dma((NM * PARTS, nw)),
            dma((2, PARTS, NP)), dma((2, PARTS, NP)),
            dma((PARTS, NP)), dma((PARTS, NP)),
            dma((nw, 2, C)), dma((nw, 2, C)),
            dma((3 + NM * PARTS,)),
        ],
        compiler_params=pltpu.CompilerParams(
            collective_id=0, has_side_effects=True, vmem_limit_bytes=56 * 1024 * 1024
        ),
    )(
        scalar_field.reshape(rows, PEN), velocity, reaction_rate,
        sample_cells.reshape(1, S), weight_in, weight_out,
    ))
    outs = tuple(pltpu.with_memory_space_constraint(o, pltpu.VMEM) for o in outs)
    return tuple(pl.pallas_call(
        finish,
        out_shape=tuple(jax.ShapeDtypeStruct(s, F32) for s in shapes),
        in_specs=[vmem] * 3,
        out_specs=(hbm,) * 3,
        scratch_shapes=[dma((3,))],
    )(*outs))


def solution(mesh):
    sizes = (mesh.shape["gx"], mesh.shape["gy"], mesh.shape["gz"])
    in_specs = (
        P("gx", "gy", "gz"),
        P(None, "gx", "gy", "gz"),
        P("gx", "gy", "gz"),
        P("gx", "gy", "gz"),
        P(("gx", "gy", "gz"), None),
        P(("gx", "gy", "gz"), None),
    )
    out_specs = (P("gx", "gy", "gz"), P(("gx", "gy", "gz"), None), P(("gx", "gy", "gz"), None))
    return jax.shard_map(
        functools.partial(shards, sizes), mesh=mesh, in_specs=in_specs, out_specs=out_specs,
        check_vma=False,
    )
```
